512 devices in a mesh: case: 32 (over z, x_hi), bx: 8 (over x_lo, y), by: 2 (over core).
Axes of the slice: x: 4 (x_hi: 2, x_lo: 2; x = x_hi * 2 + x_lo), y: 4, z: 16, core: 2. Of those that a mesh axis runs over, the one named last changes fastest.
Arguments:
- displacements: bfloat16 [64, 3, 64, 16, 256], P('case', None, 'bx', 'by'), may hold values from -6 to 6
- material_ids: int32 [64, 16, 256], P('bx', 'by'), may hold values from 0 to 7
- lame: float32 [2, 8], replicated, may hold values from 0.5 to 2
- slab_bounds: int32 [2, 64], P(None, 'bx'), may hold values from 0 to 256, as said below
- load_history: bfloat16 [1024, 64], replicated, may hold values from -0.75 to 0.75
Outputs:
- vm_peak: float32 [64, 16, 256], P('bx', 'by', 'case')
- hyd_range: float32 [64, 16, 256], P('bx', 'by', 'case')
The draws below stay inside these ranges and needn't reach their ends.
Inputs may be any that keep to these rules, and one draw needn't show every extreme that they name: `slab_bounds`: row 0 lies below 64 and row 1 above 192 for every x.
All inputs are finite; a program needn't handle non-finite values.
Results may differ from the reference program's by a relative error of at most 0.00097.
Values may be sent and summed in bfloat16 or wider, within the bound.
A program may use at most 64 MiB of HBM per device.

```python
import math
import jax
import jax.numpy as jnp
from jax import lax

NZ = 256
TIME = 1024
MATS = 8
CASES = 64
NX = 64
NY = 16


def draw_slab_bounds(key, part):
    lower_key = jax.random.fold_in(key, 11)
    upper_key = jax.random.fold_in(key, 23)
    lower = jax.random.randint(lower_key, (NX,), 0, NZ // 4, dtype=jnp.int32)
    upper = jax.random.randint(upper_key, (NX,), 3 * NZ // 4 + 1, NZ + 1, dtype=jnp.int32)
    lower = lower.at[0].set(0)
    upper = upper.at[NX - 1].set(NZ)
    return jnp.stack([lower, upper]).astype(jnp.int32)


def touch_ends(array, own_key, least, high):
    extent = array.shape
    spot = [jax.random.randint(jax.random.fold_in(own_key, axis), (), 0, extent[axis]) for axis in range(len(extent))]
    array = array.at[tuple(spot)].set(least)
    longest = extent.index(max(extent))
    spot[longest] = (spot[longest] + 1) % extent[longest]
    return array.at[tuple(spot)].set(high)


def levels(key, extent, cuts, smallest, largest):
    loudness = 1.0
    for position, shards_of in cuts:
        heights = jax.random.uniform(jax.random.fold_in(jax.random.fold_in(key, 6), position), (shards_of,), jnp.float32, smallest / len(cuts), largest / len(cuts))
        loudness = loudness * jnp.repeat(jnp.exp(heights), extent[position] // shards_of).reshape((-1,) + (1,) * (len(extent) - 1 - position))
    return loudness


def bell_draw(rng, dims, width, bound, cuts=(), kind=jnp.bfloat16):
    array = width * jax.random.normal(rng, dims, jnp.float32)
    if cuts:
        array = array * levels(rng, dims, cuts, -0.22, 0.18)
    return jnp.clip(array, -bound, bound).astype(kind)


def setup_inputs(seed: int = 0) -> dict:
    keys = jax.random.split(jax.random.key(seed), 6)
    displacements = bell_draw(keys[0], (CASES, 3, NX, NY, NZ), 1.0, 6.0, ((0, 32), (2, 8), (3, 2)))
    material_ids = touch_ends(jax.random.randint(keys[1], (NX, NY, NZ), 0, MATS), jax.random.fold_in(keys[1], 1), 0, MATS - 1).astype(jnp.int32)
    lame = jnp.clip(jnp.exp(jax.random.uniform(keys[2], (2, MATS), jnp.float32, math.log(0.5), math.log(2.0))), 0.5, 2.0)
    slab_bounds = draw_slab_bounds(jax.random.fold_in(keys[5], 71), 0)
    load_history = bell_draw(keys[4], (TIME, CASES), CASES ** -0.5, 0.75)
    return {"displacements": displacements, "material_ids": material_ids, "lame": lame, "slab_bounds": slab_bounds, "load_history": load_history}


def derivative(extended, comp, along):
    field = extended[..., comp, :, :, :]
    if along == 0:
        return 0.5 * (field[..., 2:, 1:-1, 1:-1] - field[..., :-2, 1:-1, 1:-1])
    if along == 1:
        return 0.5 * (field[..., 1:-1, 2:, 1:-1] - field[..., 1:-1, :-2, 1:-1])
    return 0.5 * (field[..., 1:-1, 1:-1, 2:] - field[..., 1:-1, 1:-1, :-2])

def stress_field(extended, shear_mod, lame_first, weight):
    extended = extended.astype(jnp.float32)
    grads = [[derivative(extended, comp, along) for along in range(3)] for comp in range(3)]
    trace = grads[0][0] + grads[1][1] + grads[2][2]
    normal_x = (lame_first * trace + 2.0 * shear_mod * grads[0][0]) * weight
    normal_y = (lame_first * trace + 2.0 * shear_mod * grads[1][1]) * weight
    normal_z = (lame_first * trace + 2.0 * shear_mod * grads[2][2]) * weight
    shear_xy = shear_mod * (grads[0][1] + grads[1][0]) * weight
    shear_yz = shear_mod * (grads[1][2] + grads[2][1]) * weight
    shear_zx = shear_mod * (grads[2][0] + grads[0][2]) * weight
    return jnp.stack([normal_x, normal_y, normal_z, shear_xy, shear_yz, shear_zx], axis=-4)

def invariants(history):
    diff_one = history[:, 0] - history[:, 1]
    diff_two = history[:, 1] - history[:, 2]
    diff_three = history[:, 2] - history[:, 0]
    mises2 = 0.5 * (diff_one * diff_one + diff_two * diff_two + diff_three * diff_three)
    mises2 = mises2 + 3.0 * (history[:, 3] * history[:, 3] + history[:, 4] * history[:, 4] + history[:, 5] * history[:, 5])
    hydro = (history[:, 0] + history[:, 1] + history[:, 2]) / 3.0
    return (mises2, hydro)

def reference(displacements, material_ids, lame, slab_bounds, load_history):
    shear_mod = lame[0][material_ids]
    lame_first = lame[1][material_ids]
    depth = jnp.arange(NZ, dtype=jnp.int32)
    inside = (slab_bounds[0][:, None] <= depth[None, :]) & (depth[None, :] < slab_bounds[1][:, None])
    weight = inside.astype(jnp.float32)[:, None, :]

    def one_case(field):
        extended = jnp.pad(field.astype(jnp.float32), ((0, 0), (1, 1), (1, 1), (1, 1)))
        return stress_field(extended, shear_mod, lame_first, weight).astype(jnp.bfloat16)
    stress = lax.map(one_case, displacements)
    factors = load_history.astype(jnp.float32)

    def per_row(index):
        sheet = lax.dynamic_index_in_dim(stress, index, 2, keepdims=False)
        flat = sheet.reshape(sheet.shape[0], -1).astype(jnp.float32)
        history = jnp.dot(factors, flat, preferred_element_type=jnp.float32).reshape(TIME, 6, NY, NZ)
        mises2, hydro = invariants(history)
        return (jnp.sqrt(lax.optimization_barrier(jnp.max(mises2, axis=0))), lax.optimization_barrier(jnp.max(hydro, axis=0)) - lax.optimization_barrier(jnp.min(hydro, axis=0)))
    vm_peak, hyd_range = lax.map(per_row, jnp.arange(NX, dtype=jnp.int32))
    return (vm_peak, hyd_range)
```

```python
import functools
import math

import jax
import jax.numpy as jnp
from jax import lax
from jax.experimental import pallas as pl
from jax.experimental.pallas import tpu as pltpu
from jax.sharding import PartitionSpec as P

MESH = pl.DeviceIdType.MESH
F32 = jnp.float32
BF16 = jnp.bfloat16


def z_offsets(chips):
    half = chips // 2
    offsets = [half]
    for distance in range(half - 1, 0, -1):
        offsets += [distance, -distance]
    return offsets + [0]


def slot_of(chips, offset, flip):
    return 2 * z_offsets(chips).index(offset) + 1 - flip


def kernel(
    chips, cuts, disp_ref, mat_ref, lame_ref, bounds_ref, hist_ref, peak_ref, range_ref,
    turned, edge, send, own, low, high, side, moduli, weights, factors, cells, rhs, rhs_shear,
    sent, got, moved, moved_sent, local,
):
    case = lax.axis_index("case")
    bx = lax.axis_index("bx")
    by = lax.axis_index("by")
    bricks = lax.axis_size("bx")
    chip_z = case // 2
    half = lax.rem(case, 2)
    slots = 2 * chips

    def peer(offset, flip):
        return lax.rem(chip_z + offset + chips, chips) * 2 + lax.rem(half + flip, 2)

    offsets = [(dz, flip) for dz in z_offsets(chips) for flip in (1, 0)][:-1]
    x_next = {"bx": lax.rem(bx + 1, bricks)}
    x_prev = {"bx": lax.rem(bx + bricks - 1, bricks)}
    partner = {"by": 1 - by}

    barrier = pltpu.get_barrier_semaphore()
    for dz, flip in offsets:
        pl.semaphore_signal(barrier, inc=1, device_id={"case": peer(dz, flip)}, device_id_type=MESH)
    for target in (x_next, x_prev, partner):
        pl.semaphore_signal(barrier, inc=1, device_id=target, device_id_type=MESH)

    zero_rows = jnp.zeros((8, 128), F32)
    for a in range(3):
        first = disp_ref[0, a].astype(F32).reshape(64, 256)
        second = disp_ref[1, a].astype(F32).reshape(64, 256)
        flat = jnp.concatenate([first, second], axis=0)
        turned[a, 0:8] = zero_rows
        turned[a, 264:272] = zero_rows
        turned[a, 8:264] = flat.T
        send[:, a] = turned[a, 8:264].reshape(slots, 8, 128).astype(BF16)
        edge[pl.ds(2 * a, slots, stride=8), :] = turned[a, pl.ds(7, slots, stride=8), :]
        edge[pl.ds(2 * a + 1, slots, stride=8), :] = turned[a, pl.ds(16, slots, stride=8), :]
    edge[pl.ds(6, slots, stride=8), :] = jnp.zeros((slots, 128), F32)
    edge[pl.ds(7, slots, stride=8), :] = jnp.zeros((slots, 128), F32)
    send[:, 3] = edge[...].reshape(slots, 8, 128).astype(BF16)

    mine = pltpu.make_async_copy(send.at[case], own.at[slots - 1], local)
    mine.start()
    pl.semaphore_wait(barrier, len(offsets) + 3)
    for dz, flip in offsets:
        target = peer(dz, flip)
        back = dz if dz == chips // 2 else -dz
        slot = slot_of(chips, back, flip)
        group = [g for g in range(len(cuts) - 1) if cuts[g] <= slot < cuts[g + 1]][0]
        pltpu.make_async_remote_copy(
            src_ref=send.at[target],
            dst_ref=own.at[slot],
            send_sem=sent,
            recv_sem=got.at[group],
            device_id={"case": target},
            device_id_type=MESH,
        ).start()

    flat = mat_ref[...].astype(F32).reshape(64, 256)
    moduli[...] = jnp.concatenate([flat, flat], axis=0).T
    phase = moduli[pl.ds(pl.multiple_of(8 * case, 8), 8), :].astype(jnp.int32)
    lane = lax.broadcasted_iota(jnp.int32, (8, 128), 1)
    level = lax.broadcasted_iota(jnp.int32, (8, 128), 0) + 8 * case
    column = (lane // 8) % 8
    shear_mod = jnp.zeros((8, 128), F32)
    lame_first = jnp.zeros((8, 128), F32)
    bottom = jnp.zeros((8, 128), jnp.int32)
    top = jnp.zeros((8, 128), jnp.int32)
    for m in range(8):
        shear_mod = jnp.where(phase == m, lame_ref[0, m], shear_mod)
        lame_first = jnp.where(phase == m, lame_ref[1, m], lame_first)
        bottom = jnp.where(column == m, bounds_ref[0, m], bottom)
        top = jnp.where(column == m, bounds_ref[1, m], top)
    weight = ((bottom <= level) & (level < top)).astype(F32)
    shear_mod = shear_mod * weight
    lame_first = lame_first * weight

    r = lax.broadcasted_iota(jnp.int32, (128, 128), 0)
    c = lax.broadcasted_iota(jnp.int32, (128, 128), 1)
    cx = (c // 8) % 8
    cy = c % 8

    def picked(plus, minus):
        return jnp.where(plus, 0.5, jnp.where(minus, -0.5, 0.0)).astype(BF16)

    never = r < 0
    has_low = jnp.full((128, 128), bx, jnp.int32) > 0
    has_high = jnp.full((128, 128), bx, jnp.int32) < bricks - 1
    upper = jnp.full((128, 128), by, jnp.int32) > 0
    weights[0:128, 0:128] = picked((r == c + 8) & (cx < 7), (r == c - 8) & (cx > 0))
    weights[0:128, 128:256] = picked((r == c + 1) & (cy < 7), (r == c - 1) & (cy > 0))
    weights[128:256, 0:128] = picked(never, (r == c + 56) & (cx == 0) & has_low)
    weights[256:384, 0:128] = picked((r == c - 56) & (cx == 7) & has_high, never)
    weights[128:256, 128:256] = jnp.zeros((128, 128), BF16)
    weights[256:384, 128:256] = jnp.zeros((128, 128), BF16)
    weights[384:512, 0:128] = jnp.zeros((128, 128), BF16)
    weights[384:512, 128:256] = picked(
        (r == c - 7) & (cy == 7) & jnp.logical_not(upper), (r == c + 7) & (cy == 0) & upper
    )

    r = lax.broadcasted_iota(jnp.int32, (64, 128), 0)
    c = lax.broadcasted_iota(jnp.int32, (64, 128), 1)
    slot = c % slots
    pair = (c // slots) % 2
    zi = slot // 2
    far = chips // 2 - (zi + 1) // 2
    dz = jnp.where(zi % 2 == 1, far, jnp.where(zi == 0, far, -far))
    source = ((chip_z + dz + chips) % chips) * 2 + (half + 1 - slot % 2) % 2
    order = (r == 2 * source + pair).astype(F32).astype(BF16)
    steps = hist_ref.shape[1]
    for begin in range(0, steps, 256):
        block = hist_ref[:, begin : begin + 256].astype(F32).T.astype(BF16)
        factors[begin : begin + 256, :] = jnp.dot(
            block, order, preferred_element_type=F32
        ).astype(BF16)

    mine.wait()
    groups = len(cuts) - 1
    forwards = []
    for g in range(groups):
        lo, hi = cuts[g], cuts[g + 1]
        arrived = own.at[pl.ds(lo, min(hi, slots - 1) - lo)]
        pltpu.make_async_remote_copy(
            src_ref=arrived, dst_ref=arrived, send_sem=sent, recv_sem=got.at[g],
            device_id=partner, device_id_type=MESH,
        ).wait_recv()
        for k, (target, place) in enumerate(((x_next, low), (x_prev, high), (partner, side))):
            move = pltpu.make_async_remote_copy(
                src_ref=own.at[pl.ds(lo, hi - lo), pl.ds(0, 3)],
                dst_ref=place.at[pl.ds(lo, hi - lo)],
                send_sem=moved_sent.at[k, g],
                recv_sem=moved.at[k, g],
                device_id=target,
                device_id_type=MESH,
            )
            move.start()
            forwards.append(move)

    row = lax.broadcasted_iota(jnp.int32, (8, 8, 128), 1)
    for g in range(groups):
        for k in range(3):
            forwards[3 * g + k].wait_recv()
        for s0 in range(cuts[g], cuts[g + 1], 8):
            here = [ref[s0 : s0 + 8, 0:3].astype(F32) for ref in (own, low, high, side)]
            flat = jnp.concatenate(
                [part.reshape(192, 128).astype(BF16) for part in here], axis=1
            )
            planar = jnp.dot(flat, weights[...], preferred_element_type=F32)
            along_x = planar[:, 0:128].reshape(8, 3, 8, 128)
            along_y = planar[:, 128:256].reshape(8, 3, 8, 128)
            halo = own[s0 : s0 + 8, 3].astype(F32)
            along_z = []
            for a in range(3):
                field = here[0][:, a]
                up = jnp.where(row == 7, halo[:, 2 * a + 1 : 2 * a + 2], pltpu.roll(field, 7, 1))
                down = jnp.where(row == 0, halo[:, 2 * a : 2 * a + 1], pltpu.roll(field, 1, 1))
                along_z.append(0.5 * (up - down))
            g_xx, g_yy, g_zz = along_x[:, 0], along_y[:, 1], along_z[2]
            spread = lame_first * (g_xx + g_yy + g_zz)
            double = 2.0 * shear_mod
            rounded = [
                value.astype(BF16).astype(F32)
                for value in (
                    spread + double * g_xx,
                    spread + double * g_yy,
                    spread + double * g_zz,
                    shear_mod * (along_y[:, 0] + along_x[:, 1]),
                    shear_mod * (along_z[1] + along_y[:, 2]),
                    shear_mod * (along_x[:, 2] + along_z[0]),
                )
            ]
            s_x, s_y, s_z = rounded[:3]
            values = [
                0.5 * (s_x - s_y),
                (s_x + s_y - 2.0 * s_z) * (0.5 / math.sqrt(3.0)),
                s_x + s_y + s_z,
            ] + rounded[3:]
            for k in range(6):
                for i in range(8):
                    cells[k, pl.ds(s0 + i, 8, stride=slots), :] = values[k][i]

    lane = lax.broadcasted_iota(jnp.int32, (slots, 128), 1)
    for k in range(6):
        for p in range(4):
            even = cells[k, 2 * p * slots : (2 * p + 1) * slots]
            odd = cells[k, (2 * p + 1) * slots : (2 * p + 2) * slots]
            first = jnp.where(lane < 64, even, pltpu.roll(odd, 64, 1))
            second = jnp.where(lane < 64, pltpu.roll(even, 64, 1), odd)
            both = jnp.concatenate([first, second], axis=0)
            coarse = both.astype(BF16)
            if k < 3:
                fine = (both - coarse.astype(F32)).astype(BF16)
                rhs[k, 0:64, 128 * p : 128 * (p + 1)] = coarse
                rhs[k, 64:128, 128 * p : 128 * (p + 1)] = fine
            else:
                rhs_shear[k - 3, :, 128 * p : 128 * (p + 1)] = coarse

    block = 256
    results = []
    for n in range(2):
        columns = slice(256 * n, 256 * (n + 1))

        def body(i, carry):
            most, upper_h, lower_h = carry
            full = factors[pl.ds(pl.multiple_of(i * block, block), block), :]
            total = None
            for k in (0, 1):
                part = jnp.dot(full, rhs[k, :, columns], preferred_element_type=F32)
                total = part * part if total is None else total + part * part
            for k in range(3):
                part = jnp.dot(full[:, 0:64], rhs_shear[k, :, columns], preferred_element_type=F32)
                total = total + part * part
            mean = jnp.dot(full, rhs[2, :, columns], preferred_element_type=F32)
            total = total.reshape(block // 8, 8, 256)
            mean = mean.reshape(block // 8, 8, 256)
            return (
                jnp.maximum(most, jnp.max(total, axis=0)),
                jnp.maximum(upper_h, jnp.max(mean, axis=0)),
                jnp.minimum(lower_h, jnp.min(mean, axis=0)),
            )

        start = (
            jnp.zeros((8, 256), F32),
            jnp.full((8, 256), -jnp.inf, F32),
            jnp.full((8, 256), jnp.inf, F32),
        )
        most, upper_h, lower_h = lax.fori_loop(0, steps // block, body, start)
        most = jnp.max(most, axis=0, keepdims=True)
        upper_h = jnp.max(upper_h, axis=0, keepdims=True)
        lower_h = jnp.min(lower_h, axis=0, keepdims=True)
        results.append((jnp.sqrt(3.0 * most), (upper_h - lower_h) * (1.0 / 3.0)))

    for which, out_ref in ((0, peak_ref), (1, range_ref)):
        rows = []
        for n in range(2):
            for p in range(2):
                pair_row = results[n][which][:, 128 * p : 128 * (p + 1)]
                rows += [pair_row, pltpu.roll(pair_row, 64, 1)]
        out_ref[...] = jnp.concatenate(rows, axis=0).T[0:64].reshape(8, 8, 8)

    whole = send.at[pl.ds(0, slots - 1)]
    pltpu.make_async_remote_copy(
        src_ref=whole, dst_ref=whole, send_sem=sent, recv_sem=got.at[0],
        device_id=partner, device_id_type=MESH,
    ).wait_send()
    for move in forwards:
        move.wait_send()


def shards(displacements, material_ids, lame, slab_bounds, load_history):
    chips = lax.axis_size("case") // 2
    slots = 2 * chips
    cuts = (0, 8, 16, 24, 32)
    groups = len(cuts) - 1
    vmem = pl.BlockSpec(memory_space=pltpu.VMEM)
    smem = pl.BlockSpec(memory_space=pltpu.SMEM)
    steps = load_history.shape[0]
    shape = jax.ShapeDtypeStruct((8, 8, 8), F32)
    return pl.pallas_call(
        functools.partial(kernel, chips, cuts),
        out_shape=(shape, shape),
        in_specs=[vmem, vmem, smem, smem, vmem],
        out_specs=(vmem, vmem),
        scratch_shapes=[
            pltpu.VMEM((3, 272, 128), F32),
            pltpu.VMEM((8 * slots, 128), F32),
            pltpu.VMEM((slots, 4, 8, 128), BF16),
            pltpu.VMEM((slots, 4, 8, 128), BF16),
            pltpu.VMEM((slots, 3, 8, 128), BF16),
            pltpu.VMEM((slots, 3, 8, 128), BF16),
            pltpu.VMEM((slots, 3, 8, 128), BF16),
            pltpu.VMEM((256, 128), F32),
            pltpu.VMEM((512, 256), BF16),
            pltpu.VMEM((steps, 128), BF16),
            pltpu.VMEM((6, 8 * slots, 128), F32),
            pltpu.VMEM((3, 128, 512), BF16),
            pltpu.VMEM((3, 64, 512), BF16),
            pltpu.SemaphoreType.DMA,
            pltpu.SemaphoreType.DMA((groups,)),
            pltpu.SemaphoreType.DMA((3, groups)),
            pltpu.SemaphoreType.DMA((3, groups)),
            pltpu.SemaphoreType.DMA,
        ],
        compiler_params=pltpu.CompilerParams(collective_id=0, has_side_effects=True),
    )(displacements, material_ids, lame, slab_bounds, load_history.T)


def solution(mesh):
    in_specs = (P("case", None, "bx", "by", None), P("bx", "by", None), P(), P(None, "bx"), P())
    out_specs = (P("bx", "by", "case"), P("bx", "by", "case"))
    return jax.shard_map(shards, mesh=mesh, in_specs=in_specs, out_specs=out_specs, check_vma=False)
```

```python
import functools
import math

import jax
import jax.numpy as jnp
from jax import lax
from jax.experimental import pallas as pl
from jax.experimental.pallas import tpu as pltpu
from jax.sharding import PartitionSpec as P

MESH = pl.DeviceIdType.MESH
F32 = jnp.float32
BF16 = jnp.bfloat16
GROUP = 8


def kernel(
    order, disp_any, mat_any, lame_any, bounds_any, hist_any, most_ref, spread_ref,
    disp_ref, mat_ref, lame_ref, bounds_ref, hist_ref, loaded,
    turned, send, own, faces, halos, rows_ref, halo_rows, moduli, weights, factors, cells, rhs, rhs_shear,
    sent, got, face_sent, face_got,
):
    case = lax.axis_index("case")
    bx = lax.axis_index("bx")
    by = lax.axis_index("by")
    bricks = lax.axis_size("bx")
    slots = lax.axis_size("case")
    x_next = {"bx": lax.rem(bx + 1, bricks)}
    x_prev = {"bx": lax.rem(bx + bricks - 1, bricks)}
    partner = {"by": 1 - by}
    above = {"case": lax.rem(case + 1, slots)}
    below = {"case": lax.rem(case + slots - 1, slots)}

    barrier = pltpu.get_barrier_semaphore()
    for target in range(slots):
        @pl.when(target != case)
        def _():
            pl.semaphore_signal(barrier, inc=1, device_id={"case": target}, device_id_type=MESH)
    for target in (x_next, x_prev, partner):
        pl.semaphore_signal(barrier, inc=1, device_id=target, device_id_type=MESH)

    loads = [
        pltpu.make_async_copy(src, dst, loaded.at[i])
        for i, (src, dst) in enumerate(
            (
                (disp_any, disp_ref),
                (hist_any, hist_ref),
                (mat_any, mat_ref),
                (lame_any, lame_ref),
                (bounds_any, bounds_ref),
            )
        )
    ]
    for load in loads:
        load.start()

    loads[0].wait()
    for a in range(3):
        first = disp_ref[0, a].astype(F32).reshape(64, 256)
        second = disp_ref[1, a].astype(F32).reshape(64, 256)
        turned[...] = jnp.concatenate([first, second], axis=0).T
        send[:, a] = turned[...].reshape(slots, 8, 128).astype(BF16)

    pl.semaphore_wait(barrier, slots + 2)
    mine = pltpu.make_async_copy(send.at[case], own.at[case], got.at[case // GROUP])
    mine.start()
    for target in range(slots):
        @pl.when(target != case)
        def _():
            pltpu.make_async_remote_copy(
                src_ref=send.at[target],
                dst_ref=own.at[case],
                send_sem=sent,
                recv_sem=got.at[case // GROUP],
                device_id={"case": target},
                device_id_type=MESH,
            ).start()

    loads[1].wait()
    r = lax.broadcasted_iota(jnp.int32, (64, 128), 0)
    c = lax.broadcasted_iota(jnp.int32, (64, 128), 1)
    permute = (r == 2 * (c % slots) + (c // slots) % 2).astype(F32).astype(BF16)
    steps = hist_ref.shape[1]
    for begin in range(0, steps, 256):
        block = hist_ref[:, begin : begin + 256].astype(F32).T.astype(BF16)
        factors[begin : begin + 256, :] = jnp.dot(
            block, permute, preferred_element_type=F32
        ).astype(BF16)

    for load in loads[2:]:
        load.wait()
    flat = mat_ref[...].astype(F32).reshape(64, 256)
    moduli[...] = jnp.concatenate([flat, flat], axis=0).T
    phase = moduli[pl.ds(pl.multiple_of(8 * case, 8), 8), :].astype(jnp.int32)
    lane = lax.broadcasted_iota(jnp.int32, (8, 128), 1)
    row = lax.broadcasted_iota(jnp.int32, (8, 128), 0)
    level = row + 8 * case
    column = (lane // 8) % 8
    shear_mod = jnp.zeros((8, 128), F32)
    lame_first = jnp.zeros((8, 128), F32)
    bottom = jnp.zeros((8, 128), jnp.int32)
    top = jnp.zeros((8, 128), jnp.int32)
    for m in range(8):
        shear_mod = jnp.where(phase == m, lame_ref[0, m], shear_mod)
        lame_first = jnp.where(phase == m, lame_ref[1, m], lame_first)
        bottom = jnp.where(column == m, bounds_ref[0, m], bottom)
        top = jnp.where(column == m, bounds_ref[1, m], top)
    weight = ((bottom <= level) & (level < top)).astype(F32)
    shear_mod = shear_mod * weight
    lame_first = lame_first * weight
    double = 2.0 * shear_mod

    r = lax.broadcasted_iota(jnp.int32, (128, 128), 0)
    c = lax.broadcasted_iota(jnp.int32, (128, 128), 1)
    cx = (c // 8) % 8
    cy = c % 8
    same = r // 64 == c // 64

    def picked(plus, minus):
        return jnp.where(plus, 0.5, jnp.where(minus, -0.5, 0.0)).astype(BF16)

    never = r < 0
    has_low = jnp.full((128, 128), bx, jnp.int32) > 0
    has_high = jnp.full((128, 128), bx, jnp.int32) < bricks - 1
    upper = jnp.full((128, 128), by, jnp.int32) > 0
    lower = jnp.full((128, 128), by, jnp.int32) < 1
    none = jnp.zeros((128, 128), BF16)
    weights[0:128, 0:128] = picked((r == c + 8) & (cx < 7), (r == c - 8) & (cx > 0))
    weights[0:128, 128:256] = picked((r == c + 1) & (cy < 7), (r == c - 1) & (cy > 0))
    weights[128:256, 0:128] = picked(never, same & (r % 8 == cy) & (cx == 0) & has_low)
    weights[256:384, 0:128] = picked(same & (r % 8 == cy) & (cx == 7) & has_high, never)
    weights[128:256, 128:256] = none
    weights[256:384, 128:256] = none
    weights[384:512, 0:128] = none
    alike = same & ((r // 8) % 8 == cx)
    weights[384:512, 128:256] = picked(alike & (cy == 7) & lower, alike & (cy == 0) & upper)

    in_upper = jnp.full((GROUP, 128), by, jnp.int32) > 0
    moves = {}

    @pl.when(case == 0)
    def _():
        halos[:, 3] = jnp.zeros(halos.shape[:1] + halos.shape[2:], BF16)

    @pl.when(case == slots - 1)
    def _():
        halos[:, 4] = jnp.zeros(halos.shape[:1] + halos.shape[2:], BF16)

    for g in order:
        s0 = GROUP * g
        arrived = own.at[pl.ds(s0, GROUP)]
        pltpu.make_async_remote_copy(
            src_ref=arrived, dst_ref=arrived, send_sem=sent, recv_sem=got.at[g],
            device_id=partner, device_id_type=MESH,
        ).wait_recv()
        rows_ref[g] = own[s0 : s0 + GROUP].astype(F32).reshape(24 * GROUP, 128)
        packed = [[], [], [], [], []]
        for a in range(3):
            to_next = to_prev = to_side = jnp.zeros((GROUP, 128), F32)
            for z in range(8):
                value = rows_ref[g, pl.ds(8 * a + z, GROUP, stride=24), :]
                to_next = jnp.where(column == z, pltpu.roll(value, (8 * z - 56) % 128, 1), to_next)
                to_prev = jnp.where(column == z, pltpu.roll(value, 8 * z, 1), to_prev)
                turn = jnp.where(in_upper, pltpu.roll(value, z, 1), pltpu.roll(value, (z - 7) % 128, 1))
                to_side = jnp.where(lane % 8 == z, turn, to_side)
                if z == 0:
                    packed[4].append(value)
                if z == 7:
                    packed[3].append(value)
            packed[0].append(to_next)
            packed[1].append(to_prev)
            packed[2].append(to_side)
        for k, target in enumerate((x_next, x_prev, partner, above, below)):
            for a in range(3):
                faces[g, k, a] = packed[k][a].astype(BF16)
            move = pltpu.make_async_remote_copy(
                src_ref=faces.at[g, k],
                dst_ref=halos.at[g, k],
                send_sem=face_sent.at[g, k],
                recv_sem=face_got.at[g, k],
                device_id=target,
                device_id_type=MESH,
            )
            moves[g, k] = move
            if k < 3:
                move.start()
            elif k == 3:
                pl.when(case < slots - 1)(move.start)
            else:
                pl.when(case > 0)(move.start)

    in_column = column == row
    in_row = lane % 8 == row
    for g in order:
        s0 = GROUP * g
        for k in range(5):
            if k < 3:
                moves[g, k].wait_recv()
            elif k == 3:
                pl.when(case > 0)(moves[g, k].wait_recv)
            else:
                pl.when(case < slots - 1)(moves[g, k].wait_recv)
            halo_rows[g, k] = halos[g, k].astype(F32).reshape(3 * GROUP, 128)

        def halo(k, i, a):
            at = GROUP * a + i
            return jnp.broadcast_to(halo_rows[g, k, at : at + 1, :], (8, 128))

        parts = [rows_ref[g]]
        for k, mask in ((0, in_column), (1, in_column), (2, in_row)):
            parts.append(
                jnp.concatenate(
                    [
                        jnp.where(mask, halo(k, i, a), 0.0)
                        for i in range(GROUP)
                        for a in range(3)
                    ],
                    axis=0,
                )
            )
        flat = jnp.concatenate([part.astype(BF16) for part in parts], axis=1)
        planar = jnp.dot(flat, weights[...], preferred_element_type=F32)
        for i in range(GROUP):
            grads = []
            for a in range(3):
                at = 24 * i + 8 * a
                field = rows_ref[g, at : at + 8]
                down = jnp.where(
                    row == 0,
                    halo(3, i, a),
                    pltpu.roll(field, 1, 0),
                )
                up = jnp.where(
                    row == 7,
                    halo(4, i, a),
                    pltpu.roll(field, 7, 0),
                )
                grads.append(
                    (planar[at : at + 8, 0:128], planar[at : at + 8, 128:256], 0.5 * (up - down))
                )
            g_xx, g_yy, g_zz = grads[0][0], grads[1][1], grads[2][2]
            spread = lame_first * (g_xx + g_yy + g_zz)
            s_x, s_y, s_z, s_xy, s_yz, s_zx = [
                value.astype(BF16).astype(F32)
                for value in (
                    spread + double * g_xx,
                    spread + double * g_yy,
                    spread + double * g_zz,
                    shear_mod * (grads[0][1] + grads[1][0]),
                    shear_mod * (grads[1][2] + grads[2][1]),
                    shear_mod * (grads[2][0] + grads[0][2]),
                )
            ]
            values = (
                0.5 * (s_x - s_y),
                (s_x + s_y - 2.0 * s_z) * (0.5 / math.sqrt(3.0)),
                s_x + s_y + s_z,
                s_xy,
                s_yz,
                s_zx,
            )
            for k in range(6):
                cells[k, pl.ds(s0 + i, 8, stride=slots), :] = values[k]

    left = lax.broadcasted_iota(jnp.int32, (slots, 128), 1) < 64
    for k in range(6):
        for p in range(4):
            even = cells[k, 2 * p * slots : (2 * p + 1) * slots]
            odd = cells[k, (2 * p + 1) * slots : (2 * p + 2) * slots]
            first = jnp.where(left, even, pltpu.roll(odd, 64, 1))
            second = jnp.where(left, pltpu.roll(even, 64, 1), odd)
            both = jnp.concatenate([first, second], axis=0)
            coarse = both.astype(BF16)
            if k < 3:
                fine = (both - coarse.astype(F32)).astype(BF16)
                rhs[k, 0:64, 128 * p : 128 * (p + 1)] = coarse
                rhs[k, 64:128, 128 * p : 128 * (p + 1)] = fine
            else:
                rhs_shear[k - 3, :, 128 * p : 128 * (p + 1)] = coarse

    block = 256
    results = []
    for n in range(2):
        columns = slice(256 * n, 256 * (n + 1))

        def body(i, carry):
            most, upper_h, lower_h = carry
            full = factors[pl.ds(pl.multiple_of(i * block, block), block), :]
            total = None
            for k in (0, 1):
                part = jnp.dot(full, rhs[k, :, columns], preferred_element_type=F32)
                total = part * part if total is None else total + part * part
            for k in range(3):
                part = jnp.dot(full[:, 0:64], rhs_shear[k, :, columns], preferred_element_type=F32)
                total = total + part * part
            mean = jnp.dot(full, rhs[2, :, columns], preferred_element_type=F32)
            total = total.reshape(block // 8, 8, 256)
            mean = mean.reshape(block // 8, 8, 256)
            return (
                jnp.maximum(most, jnp.max(total, axis=0)),
                jnp.maximum(upper_h, jnp.max(mean, axis=0)),
                jnp.minimum(lower_h, jnp.min(mean, axis=0)),
            )

        start = (
            jnp.zeros((8, 256), F32),
            jnp.full((8, 256), -jnp.inf, F32),
            jnp.full((8, 256), jnp.inf, F32),
        )
        most, upper_h, lower_h = lax.fori_loop(0, steps // block, body, start)
        most = jnp.max(most, axis=0, keepdims=True)
        upper_h = jnp.max(upper_h, axis=0, keepdims=True)
        lower_h = jnp.min(lower_h, axis=0, keepdims=True)
        results.append((most, upper_h - lower_h))

    for which, out_ref in ((0, most_ref), (1, spread_ref)):
        rows = []
        for n in range(2):
            for p in range(2):
                pair_row = results[n][which][:, 128 * p : 128 * (p + 1)]
                rows += [pair_row, pltpu.roll(pair_row, 64, 1)]
        out_ref[...] = jnp.concatenate(rows, axis=0).T[0:64].reshape(8, 8, 8)

    whole = send.at[pl.ds(0, slots - 1)]
    pltpu.make_async_remote_copy(
        src_ref=whole, dst_ref=whole, send_sem=sent, recv_sem=got.at[0],
        device_id=partner, device_id_type=MESH,
    ).wait_send()
    for (_, k), move in moves.items():
        if k < 3:
            move.wait_send()
        elif k == 3:
            pl.when(case < slots - 1)(move.wait_send)
        else:
            pl.when(case > 0)(move.wait_send)


def shards(displacements, material_ids, lame, slab_bounds, load_history):
    slots = lax.axis_size("case")
    groups = slots // GROUP
    steps = load_history.shape[0]
    anywhere = pl.BlockSpec(memory_space=pl.ANY)
    vmem = pl.BlockSpec(memory_space=pltpu.VMEM)
    shape = jax.ShapeDtypeStruct((8, 8, 8), F32)
    factors = load_history.T
    most, spread = pl.pallas_call(
        functools.partial(kernel, (0, 1, 3, 2)),
        out_shape=(shape, shape),
        in_specs=[anywhere] * 5,
        out_specs=(vmem, vmem),
        scratch_shapes=[
            pltpu.VMEM(displacements.shape, BF16),
            pltpu.VMEM(material_ids.shape, jnp.int32),
            pltpu.SMEM(lame.shape, F32),
            pltpu.SMEM(slab_bounds.shape, jnp.int32),
            pltpu.VMEM(factors.shape, BF16),
            pltpu.SemaphoreType.DMA((5,)),
            pltpu.VMEM((256, 128), F32),
            pltpu.VMEM((slots, 3, 8, 128), BF16),
            pltpu.VMEM((slots, 3, 8, 128), BF16),
            pltpu.VMEM((groups, 5, 3, GROUP, 128), BF16),
            pltpu.VMEM((groups, 5, 3, GROUP, 128), BF16),
            pltpu.VMEM((groups, 24 * GROUP, 128), F32),
            pltpu.VMEM((groups, 5, 3 * GROUP, 128), F32),
            pltpu.VMEM((256, 128), F32),
            pltpu.VMEM((512, 256), BF16),
            pltpu.VMEM((steps, 128), BF16),
            pltpu.VMEM((6, 8 * slots, 128), F32),
            pltpu.VMEM((3, 128, 512), BF16),
            pltpu.VMEM((3, 64, 512), BF16),
            pltpu.SemaphoreType.DMA,
            pltpu.SemaphoreType.DMA((groups,)),
            pltpu.SemaphoreType.DMA((groups, 5)),
            pltpu.SemaphoreType.DMA((groups, 5)),
        ],
        compiler_params=pltpu.CompilerParams(collective_id=0, has_side_effects=True),
    )(displacements, material_ids, lame, slab_bounds, factors)
    return (jnp.sqrt(3.0 * most), spread * (1.0 / 3.0))


def solution(mesh):
    in_specs = (P("case", None, "bx", "by", None), P("bx", "by", None), P(), P(None, "bx"), P())
    out_specs = (P("bx", "by", "case"), P("bx", "by", "case"))
    return jax.shard_map(shards, mesh=mesh, in_specs=in_specs, out_specs=out_specs, check_vma=False)
```

```python
import functools
import math

import jax
import jax.numpy as jnp
from jax import lax
from jax.experimental import pallas as pl
from jax.experimental.pallas import tpu as pltpu
from jax.sharding import PartitionSpec as P

MESH = pl.DeviceIdType.MESH
F32 = jnp.float32
BF16 = jnp.bfloat16
GROUP = 8


def kernel(
    order, disp_any, mat_any, lame_any, bounds_any, hist_any, most_ref, spread_ref,
    disp_ref, mat_ref, lame_ref, bounds_ref, hist_ref, loaded,
    turned, send, own, faces, halos, rows_ref, halo_rows, moduli, weights, factors, cells, rhs, rhs_shear,
    sent, got, face_sent, face_got,
):
    case = lax.axis_index("case")
    bx = lax.axis_index("bx")
    by = lax.axis_index("by")
    bricks = lax.axis_size("bx")
    slots = lax.axis_size("case")
    x_next = {"bx": lax.rem(bx + 1, bricks)}
    x_prev = {"bx": lax.rem(bx + bricks - 1, bricks)}
    partner = {"by": 1 - by}
    above = {"case": lax.rem(case + 1, slots)}
    below = {"case": lax.rem(case + slots - 1, slots)}

    barrier = pltpu.get_barrier_semaphore()
    for target in range(slots):
        @pl.when(target != case)
        def _():
            pl.semaphore_signal(barrier, inc=1, device_id={"case": target}, device_id_type=MESH)
    for target in (x_next, x_prev, partner):
        pl.semaphore_signal(barrier, inc=1, device_id=target, device_id_type=MESH)

    loads = [
        pltpu.make_async_copy(src, dst, loaded.at[i])
        for i, (src, dst) in enumerate(
            (
                (disp_any, disp_ref),
                (hist_any, hist_ref),
                (mat_any, mat_ref),
                (lame_any, lame_ref),
                (bounds_any, bounds_ref),
            )
        )
    ]
    for load in loads:
        load.start()

    loads[0].wait()
    for a in range(3):
        first = disp_ref[0, a].astype(F32).reshape(64, 256)
        second = disp_ref[1, a].astype(F32).reshape(64, 256)
        turned[...] = jnp.concatenate([first, second], axis=0).T
        send[:, a] = turned[...].reshape(slots, 8, 128).astype(BF16)

    pl.semaphore_wait(barrier, slots + 2)
    mine = pltpu.make_async_copy(send.at[case], own.at[case], got.at[case // GROUP])
    mine.start()
    for target in range(slots):
        @pl.when(target != case)
        def _():
            pltpu.make_async_remote_copy(
                src_ref=send.at[target],
                dst_ref=own.at[case],
                send_sem=sent,
                recv_sem=got.at[case // GROUP],
                device_id={"case": target},
                device_id_type=MESH,
            ).start()

    loads[1].wait()
    r = lax.broadcasted_iota(jnp.int32, (64, 128), 0)
    c = lax.broadcasted_iota(jnp.int32, (64, 128), 1)
    permute = (r == 2 * (c % slots) + (c // slots) % 2).astype(F32).astype(BF16)
    steps = hist_ref.shape[1]
    for begin in range(0, steps, 256):
        block = hist_ref[:, begin : begin + 256].astype(F32).T.astype(BF16)
        factors[begin : begin + 256, :] = jnp.dot(
            block, permute, preferred_element_type=F32
        ).astype(BF16)

    for load in loads[2:]:
        load.wait()
    flat = mat_ref[...].astype(F32).reshape(64, 256)
    moduli[...] = jnp.concatenate([flat, flat], axis=0).T
    phase = moduli[pl.ds(pl.multiple_of(8 * case, 8), 8), :].astype(jnp.int32)
    lane = lax.broadcasted_iota(jnp.int32, (8, 128), 1)
    row = lax.broadcasted_iota(jnp.int32, (8, 128), 0)
    level = row + 8 * case
    column = (lane // 8) % 8
    shear_mod = jnp.zeros((8, 128), F32)
    lame_first = jnp.zeros((8, 128), F32)
    bottom = jnp.zeros((8, 128), jnp.int32)
    top = jnp.zeros((8, 128), jnp.int32)
    for m in range(8):
        shear_mod = jnp.where(phase == m, lame_ref[0, m], shear_mod)
        lame_first = jnp.where(phase == m, lame_ref[1, m], lame_first)
        bottom = jnp.where(column == m, bounds_ref[0, m], bottom)
        top = jnp.where(column == m, bounds_ref[1, m], top)
    weight = ((bottom <= level) & (level < top)).astype(F32)
    shear_mod = shear_mod * weight
    lame_first = lame_first * weight
    double = 2.0 * shear_mod

    r = lax.broadcasted_iota(jnp.int32, (128, 128), 0)
    c = lax.broadcasted_iota(jnp.int32, (128, 128), 1)
    cx = (c // 8) % 8
    cy = c % 8
    same = r // 64 == c // 64

    def picked(plus, minus):
        return jnp.where(plus, 0.5, jnp.where(minus, -0.5, 0.0)).astype(BF16)

    never = r < 0
    has_low = jnp.full((128, 128), bx, jnp.int32) > 0
    has_high = jnp.full((128, 128), bx, jnp.int32) < bricks - 1
    upper = jnp.full((128, 128), by, jnp.int32) > 0
    lower = jnp.full((128, 128), by, jnp.int32) < 1
    none = jnp.zeros((128, 128), BF16)
    weights[0:128, 0:128] = picked((r == c + 8) & (cx < 7), (r == c - 8) & (cx > 0))
    weights[0:128, 128:256] = picked((r == c + 1) & (cy < 7), (r == c - 1) & (cy > 0))
    weights[128:256, 0:128] = picked(never, same & (r % 8 == cy) & (cx == 0) & has_low)
    weights[256:384, 0:128] = picked(same & (r % 8 == cy) & (cx == 7) & has_high, never)
    weights[128:256, 128:256] = none
    weights[256:384, 128:256] = none
    weights[384:512, 0:128] = none
    alike = same & ((r // 8) % 8 == cx)
    weights[384:512, 128:256] = picked(alike & (cy == 7) & lower, alike & (cy == 0) & upper)

    in_upper = jnp.full((GROUP, 128), by, jnp.int32) > 0
    moves = {}

    @pl.when(case == 0)
    def _():
        halos[:, 3] = jnp.zeros(halos.shape[:1] + halos.shape[2:], BF16)

    @pl.when(case == slots - 1)
    def _():
        halos[:, 4] = jnp.zeros(halos.shape[:1] + halos.shape[2:], BF16)

    for g in order:
        s0 = GROUP * g
        arrived = own.at[pl.ds(s0, GROUP)]
        pltpu.make_async_remote_copy(
            src_ref=arrived, dst_ref=arrived, send_sem=sent, recv_sem=got.at[g],
            device_id=partner, device_id_type=MESH,
        ).wait_recv()
        rows_ref[g] = own[s0 : s0 + GROUP].astype(F32).reshape(24 * GROUP, 128)
        packed = [[], [], [], [], []]
        for a in range(3):
            to_next = to_prev = to_side = jnp.zeros((GROUP, 128), F32)
            for z in range(8):
                value = rows_ref[g, pl.ds(8 * a + z, GROUP, stride=24), :]
                to_next = jnp.where(column == z, pltpu.roll(value, (8 * z - 56) % 128, 1), to_next)
                to_prev = jnp.where(column == z, pltpu.roll(value, 8 * z, 1), to_prev)
                turn = jnp.where(in_upper, pltpu.roll(value, z, 1), pltpu.roll(value, (z - 7) % 128, 1))
                to_side = jnp.where(lane % 8 == z, turn, to_side)
                if z == 0:
                    packed[4].append(value)
                if z == 7:
                    packed[3].append(value)
            packed[0].append(to_next)
            packed[1].append(to_prev)
            packed[2].append(to_side)
        for k, target in enumerate((x_next, x_prev, partner, above, below)):
            for a in range(3):
                faces[g, k, a] = packed[k][a].astype(BF16)
            move = pltpu.make_async_remote_copy(
                src_ref=faces.at[g, k],
                dst_ref=halos.at[g, k],
                send_sem=face_sent.at[g, k],
                recv_sem=face_got.at[g, k],
                device_id=target,
                device_id_type=MESH,
            )
            moves[g, k] = move
            if k < 3:
                move.start()
            elif k == 3:
                pl.when(case < slots - 1)(move.start)
            else:
                pl.when(case > 0)(move.start)

    in_column = column == row
    in_row = lane % 8 == row
    for g in order:
        s0 = GROUP * g
        for k in range(5):
            if k < 3:
                moves[g, k].wait_recv()
            elif k == 3:
                pl.when(case > 0)(moves[g, k].wait_recv)
            else:
                pl.when(case < slots - 1)(moves[g, k].wait_recv)
            halo_rows[g, k] = halos[g, k].astype(F32).reshape(3 * GROUP, 128)

        def halo(k, i, a):
            at = GROUP * a + i
            return jnp.broadcast_to(halo_rows[g, k, at : at + 1, :], (8, 128))

        parts = [rows_ref[g]]
        for k, mask in ((0, in_column), (1, in_column), (2, in_row)):
            parts.append(
                jnp.concatenate(
                    [
                        jnp.where(mask, halo(k, i, a), 0.0)
                        for i in range(GROUP)
                        for a in range(3)
                    ],
                    axis=0,
                )
            )
        flat = jnp.concatenate([part.astype(BF16) for part in parts], axis=1)
        planar = jnp.dot(flat, weights[...], preferred_element_type=F32)
        for i in range(GROUP):
            grads = []
            for a in range(3):
                at = 24 * i + 8 * a
                field = rows_ref[g, at : at + 8]
                down = jnp.where(
                    row == 0,
                    halo(3, i, a),
                    pltpu.roll(field, 1, 0),
                )
                up = jnp.where(
                    row == 7,
                    halo(4, i, a),
                    pltpu.roll(field, 7, 0),
                )
                grads.append(
                    (planar[at : at + 8, 0:128], planar[at : at + 8, 128:256], 0.5 * (up - down))
                )
            g_xx, g_yy, g_zz = grads[0][0], grads[1][1], grads[2][2]
            spread = lame_first * (g_xx + g_yy + g_zz)
            s_x, s_y, s_z, s_xy, s_yz, s_zx = [
                value.astype(BF16).astype(F32)
                for value in (
                    spread + double * g_xx,
                    spread + double * g_yy,
                    spread + double * g_zz,
                    shear_mod * (grads[0][1] + grads[1][0]),
                    shear_mod * (grads[1][2] + grads[2][1]),
                    shear_mod * (grads[2][0] + grads[0][2]),
                )
            ]
            values = (
                0.5 * (s_x - s_y),
                (s_x + s_y - 2.0 * s_z) * (0.5 / math.sqrt(3.0)),
                s_x + s_y + s_z,
                s_xy,
                s_yz,
                s_zx,
            )
            for k in range(6):
                cells[k, pl.ds(s0 + i, 8, stride=slots), :] = values[k]

    left = lax.broadcasted_iota(jnp.int32, (slots, 128), 1) < 64
    for k in range(6):
        for p in range(4):
            even = cells[k, 2 * p * slots : (2 * p + 1) * slots]
            odd = cells[k, (2 * p + 1) * slots : (2 * p + 2) * slots]
            first = jnp.where(left, even, pltpu.roll(odd, 64, 1))
            second = jnp.where(left, pltpu.roll(even, 64, 1), odd)
            both = jnp.concatenate([first, second], axis=0)
            coarse = both.astype(BF16)
            if k < 3:
                fine = (both - coarse.astype(F32)).astype(BF16)
                rhs[k, 0:64, 128 * p : 128 * (p + 1)] = coarse
                rhs[k, 64:128, 128 * p : 128 * (p + 1)] = fine
            else:
                rhs_shear[k - 3, :, 128 * p : 128 * (p + 1)] = coarse

    block = 256
    results = []
    for n in range(2):
        columns = slice(256 * n, 256 * (n + 1))

        def body(i, carry):
            most, upper_h, lower_h = carry
            full = factors[pl.ds(pl.multiple_of(i * block, block), block), :]
            total = None
            for k in (0, 1):
                part = jnp.dot(full, rhs[k, :, columns], preferred_element_type=F32)
                total = part * part if total is None else total + part * part
            for k in range(3):
                part = jnp.dot(full[:, 0:64], rhs_shear[k, :, columns], preferred_element_type=F32)
                total = total + part * part
            mean = jnp.dot(full, rhs[2, :, columns], preferred_element_type=F32)
            total = total.reshape(block // 8, 8, 256)
            mean = mean.reshape(block // 8, 8, 256)
            return (
                jnp.maximum(most, jnp.max(total, axis=0)),
                jnp.maximum(upper_h, jnp.max(mean, axis=0)),
                jnp.minimum(lower_h, jnp.min(mean, axis=0)),
            )

        start = (
            jnp.zeros((8, 256), F32),
            jnp.full((8, 256), -jnp.inf, F32),
            jnp.full((8, 256), jnp.inf, F32),
        )
        most, upper_h, lower_h = lax.fori_loop(0, steps // block, body, start)
        most = jnp.max(most, axis=0, keepdims=True)
        upper_h = jnp.max(upper_h, axis=0, keepdims=True)
        lower_h = jnp.min(lower_h, axis=0, keepdims=True)
        results.append((most, upper_h - lower_h))

    for which, out_ref in ((0, most_ref), (1, spread_ref)):
        rows = []
        for n in range(2):
            for p in range(2):
                pair_row = results[n][which][:, 128 * p : 128 * (p + 1)]
                rows += [pair_row, pltpu.roll(pair_row, 64, 1)]
        out_ref[...] = jnp.concatenate(rows, axis=0).T[0:64].reshape(8, 8, 8)

    whole = send.at[pl.ds(0, slots - 1)]
    pltpu.make_async_remote_copy(
        src_ref=whole, dst_ref=whole, send_sem=sent, recv_sem=got.at[0],
        device_id=partner, device_id_type=MESH,
    ).wait_send()
    for (_, k), move in moves.items():
        if k < 3:
            move.wait_send()
        elif k == 3:
            pl.when(case < slots - 1)(move.wait_send)
        else:
            pl.when(case > 0)(move.wait_send)


def shards(displacements, material_ids, lame, slab_bounds, load_history):
    slots = lax.axis_size("case")
    groups = slots // GROUP
    steps = load_history.shape[0]
    anywhere = pl.BlockSpec(memory_space=pl.ANY)
    vmem = pl.BlockSpec(memory_space=pltpu.VMEM)
    shape = jax.ShapeDtypeStruct((8, 8, 8), F32)
    factors = load_history.T
    most, spread = pl.pallas_call(
        functools.partial(kernel, (0, 1, 3, 2)),
        out_shape=(shape, shape),
        in_specs=[anywhere] * 5,
        out_specs=(vmem, vmem),
        scratch_shapes=[
            pltpu.VMEM(displacements.shape, BF16),
            pltpu.VMEM(material_ids.shape, jnp.int32),
            pltpu.SMEM(lame.shape, F32),
            pltpu.SMEM(slab_bounds.shape, jnp.int32),
            pltpu.VMEM(factors.shape, BF16),
            pltpu.SemaphoreType.DMA((5,)),
            pltpu.VMEM((256, 128), F32),
            pltpu.VMEM((slots, 3, 8, 128), BF16),
            pltpu.VMEM((slots, 3, 8, 128), BF16),
            pltpu.VMEM((groups, 5, 3, GROUP, 128), BF16),
            pltpu.VMEM((groups, 5, 3, GROUP, 128), BF16),
            pltpu.VMEM((groups, 24 * GROUP, 128), F32),
            pltpu.VMEM((groups, 5, 3 * GROUP, 128), F32),
            pltpu.VMEM((256, 128), F32),
            pltpu.VMEM((512, 256), BF16),
            pltpu.VMEM((steps, 128), BF16),
            pltpu.VMEM((6, 8 * slots, 128), F32),
            pltpu.VMEM((3, 128, 512), BF16),
            pltpu.VMEM((3, 64, 512), BF16),
            pltpu.SemaphoreType.DMA,
            pltpu.SemaphoreType.DMA((groups,)),
            pltpu.SemaphoreType.DMA((groups, 5)),
            pltpu.SemaphoreType.DMA((groups, 5)),
        ],
        compiler_params=pltpu.CompilerParams(collective_id=0, has_side_effects=True, vmem_limit_bytes=32768 * 1024),

    )(*[pltpu.with_memory_space_constraint(v, pltpu.MemorySpace.HBM) for v in (displacements, material_ids, lame, slab_bounds, factors)])
    return (jnp.sqrt(3.0 * most), spread * (1.0 / 3.0))


def solution(mesh):
    in_specs = (P("case", None, "bx", "by", None), P("bx", "by", None), P(), P(None, "bx"), P())
    out_specs = (P("bx", "by", "case"), P("bx", "by", "case"))
    return jax.shard_map(shards, mesh=mesh, in_specs=in_specs, out_specs=out_specs, check_vma=False)
```

```python
import functools
import math

import jax
import jax.numpy as jnp
from jax import lax
from jax.experimental import pallas as pl
from jax.experimental.pallas import tpu as pltpu
from jax.sharding import PartitionSpec as P

MESH = pl.DeviceIdType.MESH
F32 = jnp.float32
BF16 = jnp.bfloat16
GROUP = 8
BLOCK = 256


def kernel(
    order, disp_any, mat_any, lame_any, bounds_any, hist_any, most_ref, spread_ref,
    disp_ref, mat_ref, lame_ref, bounds_ref, hist_ref, loaded,
    turned, send, own, faces, halos, rows_ref, halo_rows, moduli, weights, factors, cells,
    rhs_in, shear_in, rhs_two, shear_two, rhs_out, shear_out, factors_two, factors_shear,
    sent, got, face_sent, face_got,
):
    case = lax.axis_index("case")
    bx = lax.axis_index("bx")
    by = lax.axis_index("by")
    bricks = lax.axis_size("bx")
    slots = lax.axis_size("case")
    x_next = {"bx": lax.rem(bx + 1, bricks)}
    x_prev = {"bx": lax.rem(bx + bricks - 1, bricks)}
    partner = {"by": 1 - by}
    groups = slots // GROUP
    group = case // GROUP

    def relative(source, target):
        return lax.rem(source - target + groups, groups)

    above = {"case": lax.rem(case + 1, slots)}
    below = {"case": lax.rem(case + slots - 1, slots)}

    barrier = pltpu.get_barrier_semaphore()
    for target in range(slots):
        @pl.when(target != case)
        def _():
            pl.semaphore_signal(barrier, inc=1, device_id={"case": target}, device_id_type=MESH)
    for target in (x_next, x_prev, partner):
        pl.semaphore_signal(barrier, inc=1, device_id=target, device_id_type=MESH)

    loads = [
        pltpu.make_async_copy(src, dst, loaded.at[i])
        for i, (src, dst) in enumerate(
            (
                (disp_any, disp_ref),
                (hist_any, hist_ref),
                (mat_any, mat_ref),
                (lame_any, lame_ref),
                (bounds_any, bounds_ref),
            )
        )
    ]
    for load in loads:
        load.start()

    loads[0].wait()
    for a in range(3):
        first = disp_ref[0, a].astype(F32).reshape(64, 256)
        second = disp_ref[1, a].astype(F32).reshape(64, 256)
        turned[...] = jnp.concatenate([first, second], axis=0).T
        send[:, a] = turned[...].reshape(slots, 8, 128).astype(BF16)

    pl.semaphore_wait(barrier, slots + 2)
    mine = pltpu.make_async_copy(send.at[case], own.at[lax.rem(case, GROUP)], got.at[0])
    mine.start()
    for target in range(slots):
        @pl.when(target != case)
        def _():
            place = relative(group, target // GROUP)
            pltpu.make_async_remote_copy(
                src_ref=send.at[target],
                dst_ref=own.at[place * GROUP + lax.rem(case, GROUP)],
                send_sem=sent,
                recv_sem=got.at[place],
                device_id={"case": target},
                device_id_type=MESH,
            ).start()

    loads[1].wait()
    r = lax.broadcasted_iota(jnp.int32, (64, 128), 0)
    c = lax.broadcasted_iota(jnp.int32, (64, 128), 1)
    source = (c // (2 * GROUP) + group) % groups * GROUP + c % GROUP
    permute = (r == 2 * source + (c // GROUP) % 2).astype(F32).astype(BF16)
    steps = hist_ref.shape[1]
    for begin in range(0, steps, 256):
        block = hist_ref[:, begin : begin + 256].astype(F32).T.astype(BF16)
        factors[begin : begin + 256, :] = jnp.dot(
            block, permute, preferred_element_type=F32
        ).astype(BF16)

    half = steps // 2
    near = lax.broadcasted_iota(jnp.int32, (half, 128), 1) < 64
    early, late = factors[0:half, :], factors[half:steps, :]
    factors_two[:, 0:128] = early
    factors_two[:, 128:256] = late
    factors_shear[...] = jnp.where(near, early.astype(F32), late.astype(F32)).astype(BF16)
    rhs_two[...] = jnp.zeros(rhs_two.shape, BF16)
    shear_two[...] = jnp.zeros(shear_two.shape, BF16)

    for load in loads[2:]:
        load.wait()
    flat = mat_ref[...].astype(F32).reshape(64, 256)
    moduli[...] = jnp.concatenate([flat, flat], axis=0).T
    phase = moduli[pl.ds(pl.multiple_of(8 * case, 8), 8), :].astype(jnp.int32)
    lane = lax.broadcasted_iota(jnp.int32, (8, 128), 1)
    row = lax.broadcasted_iota(jnp.int32, (8, 128), 0)
    level = row + 8 * case
    column = (lane // 8) % 8
    shear_mod = jnp.zeros((8, 128), F32)
    lame_first = jnp.zeros((8, 128), F32)
    bottom = jnp.zeros((8, 128), jnp.int32)
    top = jnp.zeros((8, 128), jnp.int32)
    for m in range(8):
        shear_mod = jnp.where(phase == m, lame_ref[0, m], shear_mod)
        lame_first = jnp.where(phase == m, lame_ref[1, m], lame_first)
        bottom = jnp.where(column == m, bounds_ref[0, m], bottom)
        top = jnp.where(column == m, bounds_ref[1, m], top)
    weight = ((bottom <= level) & (level < top)).astype(F32)
    shear_mod = shear_mod * weight
    lame_first = lame_first * weight
    double = 2.0 * shear_mod

    r = lax.broadcasted_iota(jnp.int32, (128, 128), 0)
    c = lax.broadcasted_iota(jnp.int32, (128, 128), 1)
    cx = (c // 8) % 8
    cy = c % 8
    same = r // 64 == c // 64

    def picked(plus, minus):
        return jnp.where(plus, 0.5, jnp.where(minus, -0.5, 0.0)).astype(BF16)

    never = r < 0
    has_low = jnp.full((128, 128), bx, jnp.int32) > 0
    has_high = jnp.full((128, 128), bx, jnp.int32) < bricks - 1
    upper = jnp.full((128, 128), by, jnp.int32) > 0
    lower = jnp.full((128, 128), by, jnp.int32) < 1
    none = jnp.zeros((128, 128), BF16)
    weights[0:128, 0:128] = picked((r == c + 8) & (cx < 7), (r == c - 8) & (cx > 0))
    weights[0:128, 128:256] = picked((r == c + 1) & (cy < 7), (r == c - 1) & (cy > 0))
    alike = same & ((r // 8) % 8 == cx)
    weights[128:256, 0:128] = none
    weights[128:256, 128:256] = picked(alike & (cy == 7) & lower, alike & (cy == 0) & upper)
    weights[256:384, 0:128] = picked(never, same & (r % 8 == cy) & (cx == 0) & has_low)
    weights[384:512, 0:128] = picked(same & (r % 8 == cy) & (cx == 7) & has_high, never)
    weights[256:512, 128:256] = jnp.zeros((256, 128), BF16)

    in_upper = jnp.full((GROUP, 128), by, jnp.int32) > 0
    moves = {}

    @pl.when(case == 0)
    def _():
        halos[:, 3] = jnp.zeros(halos.shape[:1] + halos.shape[2:], BF16)

    @pl.when(case == slots - 1)
    def _():
        halos[:, 4] = jnp.zeros(halos.shape[:1] + halos.shape[2:], BF16)

    for g in order:
        s0 = GROUP * g
        arrived = own.at[pl.ds(s0, GROUP)]
        pltpu.make_async_remote_copy(
            src_ref=arrived, dst_ref=arrived, send_sem=sent, recv_sem=got.at[g],
            device_id=partner, device_id_type=MESH,
        ).wait_recv()
        rows_ref[g] = own[s0 : s0 + GROUP].astype(F32).reshape(24 * GROUP, 128)
        packed = [[], [], [], [], []]
        for a in range(3):
            to_next = to_prev = to_side = jnp.zeros((GROUP, 128), F32)
            for z in range(8):
                value = rows_ref[g, pl.ds(8 * a + z, GROUP, stride=24), :]
                to_next = jnp.where(column == z, pltpu.roll(value, (8 * z - 56) % 128, 1), to_next)
                to_prev = jnp.where(column == z, pltpu.roll(value, 8 * z, 1), to_prev)
                turn = jnp.where(in_upper, pltpu.roll(value, z, 1), pltpu.roll(value, (z - 7) % 128, 1))
                to_side = jnp.where(lane % 8 == z, turn, to_side)
                if z == 0:
                    packed[4].append(value)
                if z == 7:
                    packed[3].append(value)
            packed[0].append(to_next)
            packed[1].append(to_prev)
            packed[2].append(to_side)
        for k, target in enumerate((x_next, x_prev, partner, above, below)):
            for a in range(3):
                faces[g, k, a] = packed[k][a].astype(BF16)
            place = g
            if k >= 3:
                place = lax.rem(g + relative(group, target["case"] // GROUP), groups)
            move = pltpu.make_async_remote_copy(
                src_ref=faces.at[g, k],
                dst_ref=halos.at[place, k],
                send_sem=face_sent.at[g, k],
                recv_sem=face_got.at[place, k],
                device_id=target,
                device_id_type=MESH,
            )
            moves[g, k] = move
            if k < 3:
                move.start()
            elif k == 3:
                pl.when(case < slots - 1)(move.start)
            else:
                pl.when(case > 0)(move.start)

    in_column = column == row
    in_row = lane % 8 == row
    left = lane < 64

    def fetch(g, kinds):
        for k in kinds:
            arrival = pltpu.make_async_remote_copy(
                src_ref=faces.at[g, k], dst_ref=halos.at[g, k], send_sem=face_sent.at[g, k],
                recv_sem=face_got.at[g, k], device_id=partner, device_id_type=MESH,
            ).wait_recv
            if k < 3:
                arrival()
            elif k == 3:
                pl.when(case > 0)(arrival)
            else:
                pl.when(case < slots - 1)(arrival)
            halo_rows[g, k] = halos[g, k].astype(F32).reshape(3 * GROUP, 128)

    def stresses(g, full):
        def halo(k, i, a):
            at = GROUP * a + i
            return jnp.broadcast_to(halo_rows[g, k, at : at + 1, :], (8, 128))

        parts = [rows_ref[g]]
        for k, mask in ((2, in_row), (0, in_column), (1, in_column))[: 3 if full else 1]:
            parts.append(
                jnp.concatenate(
                    [
                        jnp.where(mask, halo(k, i, a), 0.0)
                        for i in range(GROUP)
                        for a in range(3)
                    ],
                    axis=0,
                )
            )
        flat = jnp.concatenate([part.astype(BF16) for part in parts], axis=1)
        planar = jnp.dot(flat, weights[0 : flat.shape[1], :], preferred_element_type=F32)
        for i in range(GROUP):
            grads = []
            for a in range(3):
                at = 24 * i + 8 * a
                field = rows_ref[g, at : at + 8]
                down = pltpu.roll(field, 1, 0)
                up = pltpu.roll(field, 7, 0)
                if full:
                    down = jnp.where(row == 0, halo(3, i, a), down)
                    up = jnp.where(row == 7, halo(4, i, a), up)
                grads.append(
                    (planar[at : at + 8, 0:128], planar[at : at + 8, 128:256], 0.5 * (up - down))
                )
            g_xx, g_yy, g_zz = grads[0][0], grads[1][1], grads[2][2]
            spread = lame_first * (g_xx + g_yy + g_zz)
            s_x, s_y, s_z, s_xy, s_yz, s_zx = [
                value.astype(BF16).astype(F32)
                for value in (
                    spread + double * g_xx,
                    spread + double * g_yy,
                    spread + double * g_zz,
                    shear_mod * (grads[0][1] + grads[1][0]),
                    shear_mod * (grads[1][2] + grads[2][1]),
                    shear_mod * (grads[2][0] + grads[0][2]),
                )
            ]
            values = (
                0.5 * (s_x - s_y),
                (s_x + s_y - 2.0 * s_z) * (0.5 / math.sqrt(3.0)),
                s_x + s_y + s_z,
                s_xy,
                s_yz,
                s_zx,
            )
            for k in range(6):
                cells[g, k, pl.ds(i, 8, stride=GROUP), :] = values[k]

    def level_of(g, k, z):
        return cells[g, k, GROUP * z : GROUP * (z + 1)]

    def keep(g, k, first, second, normal_ref, shear_ref, spots):
        both = jnp.concatenate([first, second], axis=0)
        coarse = both.astype(BF16)
        fine = (both - coarse.astype(F32)).astype(BF16)
        rows_here = 2 * GROUP
        for down, at in spots:
            begin = rows_here * g + down * (2 if k < 3 else 1)
            if k < 3:
                normal_ref[k, begin : begin + rows_here, at : at + 128] = coarse
                normal_ref[k, 64 + begin : 64 + begin + rows_here, at : at + 128] = fine
            else:
                shear_ref[k - 3, begin : begin + rows_here, at : at + 128] = coarse

    def pair_up(g, k, z_first, z_second, normal_ref, shear_ref, spots):
        one, two = level_of(g, k, z_first), level_of(g, k, z_second)
        first = jnp.where(left, one, pltpu.roll(two, 64, 1))
        second = jnp.where(left, pltpu.roll(one, 64, 1), two)
        keep(g, k, first, second, normal_ref, shear_ref, spots)

    def inner_columns(g):
        for k in range(6):
            pair_up(g, k, 1, 2, rhs_in, shear_in, ((0, 0),))
            pair_up(g, k, 3, 4, rhs_in, shear_in, ((0, 128),))
            pair_up(g, k, 5, 6, rhs_two, shear_two, ((0, 0), (64, 128)))

    def outer_columns(g):
        for k in range(6):
            pair_up(g, k, 0, 7, rhs_out, shear_out, ((0, 0),))
            first = second = jnp.zeros((GROUP, 128), F32)
            for z in range(1, 7):
                one = level_of(g, k, z)
                for side in range(2):
                    here = lane // 8 == 8 * side + z
                    turn = 8 * z + 8 * side
                    first = jnp.where(here, pltpu.roll(one, turn % 128, 1), first)
                    second = jnp.where(here, pltpu.roll(one, (turn - 64) % 128, 1), second)
            keep(g, k, first, second, rhs_out, shear_out, ((0, 128),))

    def extremes(lhs_ref, lhs_shear_ref, normal_ref, shear_ref):
        width = 256
        deep = shear_ref.shape[1]

        def body(i, carry):
            most, upper_h, lower_h = carry
            here = pl.ds(pl.multiple_of(i * BLOCK, BLOCK), BLOCK)
            full = lhs_ref[here, :]
            thin = lhs_shear_ref[here, 0:deep]
            total = None
            for k in (0, 1):
                part = jnp.dot(full, normal_ref[k], preferred_element_type=F32)
                total = part * part if total is None else total + part * part
            for k in range(3):
                part = jnp.dot(thin, shear_ref[k], preferred_element_type=F32)
                total = total + part * part
            mean = jnp.dot(full, normal_ref[2], preferred_element_type=F32)
            total = total.reshape(BLOCK // 8, 8, width)
            mean = mean.reshape(BLOCK // 8, 8, width)
            return (
                jnp.maximum(most, jnp.max(total, axis=0)),
                jnp.maximum(upper_h, jnp.max(mean, axis=0)),
                jnp.minimum(lower_h, jnp.min(mean, axis=0)),
            )

        start = (
            jnp.zeros((8, width), F32),
            jnp.full((8, width), -jnp.inf, F32),
            jnp.full((8, width), jnp.inf, F32),
        )
        most, upper_h, lower_h = lax.fori_loop(0, lhs_ref.shape[0] // BLOCK, body, start)
        most = jnp.max(most, axis=0, keepdims=True)
        upper_h = jnp.max(upper_h, axis=0, keepdims=True)
        lower_h = jnp.min(lower_h, axis=0, keepdims=True)
        return (most, upper_h, lower_h)

    for g in order:
        fetch(g, (2,))
        stresses(g, False)
        inner_columns(g)
    most, upper_h, lower_h = extremes(factors, factors, rhs_in, shear_in)
    inner = [(most, upper_h - lower_h)]
    most, upper_h, lower_h = extremes(factors_two, factors_shear, rhs_two, shear_two)
    inner.append(
        (
            jnp.maximum(most[:, 0:128], most[:, 128:256]),
            jnp.maximum(upper_h[:, 0:128], upper_h[:, 128:256])
            - jnp.minimum(lower_h[:, 0:128], lower_h[:, 128:256]),
        )
    )
    for g in order:
        fetch(g, (0, 1, 3, 4))
        stresses(g, True)
        outer_columns(g)
    most, upper_h, lower_h = extremes(factors, factors, rhs_out, shear_out)
    outer = (most, upper_h - lower_h)

    spot = lax.broadcasted_iota(jnp.int32, (1, 128), 1)
    for which, out_ref in ((0, most_ref), (1, spread_ref)):
        ends = outer[which][:, 0:128]
        sides = outer[which][:, 128:256]
        pairs = [inner[0][which][:, 0:128], inner[0][which][:, 128:256], inner[1][which]]
        rows = [ends]
        for z in range(1, 7):
            line = pairs[(z - 1) // 2]
            if z % 2 == 0:
                line = pltpu.roll(line, 64, 1)
            line = jnp.where(spot < 8, pltpu.roll(sides, -8 * z % 128, 1), line)
            line = jnp.where(spot >= 56, pltpu.roll(sides, (-8 * z - 8) % 128, 1), line)
            rows.append(line)
        rows.append(pltpu.roll(ends, 64, 1))
        out_ref[...] = jnp.concatenate(rows, axis=0).T[0:64].reshape(8, 8, 8)

    whole = send.at[pl.ds(0, slots - 1)]
    pltpu.make_async_remote_copy(
        src_ref=whole, dst_ref=whole, send_sem=sent, recv_sem=got.at[0],
        device_id=partner, device_id_type=MESH,
    ).wait_send()
    for (_, k), move in moves.items():
        if k < 3:
            move.wait_send()
        elif k == 3:
            pl.when(case < slots - 1)(move.wait_send)
        else:
            pl.when(case > 0)(move.wait_send)


def shards(displacements, material_ids, lame, slab_bounds, load_history):
    slots = lax.axis_size("case")
    groups = slots // GROUP
    steps = load_history.shape[0]
    anywhere = pl.BlockSpec(memory_space=pl.ANY)
    vmem = pl.BlockSpec(memory_space=pltpu.VMEM)
    shape = jax.ShapeDtypeStruct((8, 8, 8), F32)
    factors = load_history.T
    most, spread = pl.pallas_call(
        functools.partial(kernel, (0, 1, 3, 2)),
        out_shape=(shape, shape),
        in_specs=[anywhere] * 5,
        out_specs=(vmem, vmem),
        scratch_shapes=[
            pltpu.VMEM(displacements.shape, BF16),
            pltpu.VMEM(material_ids.shape, jnp.int32),
            pltpu.SMEM(lame.shape, F32),
            pltpu.SMEM(slab_bounds.shape, jnp.int32),
            pltpu.VMEM(factors.shape, BF16),
            pltpu.SemaphoreType.DMA((5,)),
            pltpu.VMEM((256, 128), F32),
            pltpu.VMEM((slots, 3, 8, 128), BF16),
            pltpu.VMEM((slots, 3, 8, 128), BF16),
            pltpu.VMEM((groups, 5, 3, GROUP, 128), BF16),
            pltpu.VMEM((groups, 5, 3, GROUP, 128), BF16),
            pltpu.VMEM((groups, 24 * GROUP, 128), F32),
            pltpu.VMEM((groups, 5, 3 * GROUP, 128), F32),
            pltpu.VMEM((256, 128), F32),
            pltpu.VMEM((512, 256), BF16),
            pltpu.VMEM((steps, 128), BF16),
            pltpu.VMEM((groups, 6, 8 * GROUP, 128), F32),
            pltpu.VMEM((3, 128, 256), BF16),
            pltpu.VMEM((3, 64, 256), BF16),
            pltpu.VMEM((3, 256, 256), BF16),
            pltpu.VMEM((3, 128, 256), BF16),
            pltpu.VMEM((3, 128, 256), BF16),
            pltpu.VMEM((3, 64, 256), BF16),
            pltpu.VMEM((steps // 2, 256), BF16),
            pltpu.VMEM((steps // 2, 128), BF16),
            pltpu.SemaphoreType.DMA,
            pltpu.SemaphoreType.DMA((groups,)),
            pltpu.SemaphoreType.DMA((groups, 5)),
            pltpu.SemaphoreType.DMA((groups, 5)),
        ],
        compiler_params=pltpu.CompilerParams(collective_id=0, has_side_effects=True, vmem_limit_bytes=32768 * 1024),

    )(*[pltpu.with_memory_space_constraint(v, pltpu.MemorySpace.HBM) for v in (displacements, material_ids, lame, slab_bounds, factors)])
    return (jnp.sqrt(3.0 * most), spread * (1.0 / 3.0))


def solution(mesh):
    in_specs = (P("case", None, "bx", "by", None), P("bx", "by", None), P(), P(None, "bx"), P())
    out_specs = (P("bx", "by", "case"), P("bx", "by", "case"))
    return jax.shard_map(shards, mesh=mesh, in_specs=in_specs, out_specs=out_specs, check_vma=False)
```

```python
import functools
import math

import jax
import jax.numpy as jnp
from jax import lax
from jax.experimental import pallas as pl
from jax.experimental.pallas import tpu as pltpu
from jax.sharding import PartitionSpec as P

MESH = pl.DeviceIdType.MESH
F32 = jnp.float32
BF16 = jnp.bfloat16
GROUP = 8
BLOCK = 1024


def kernel(
    order, disp_any, mat_any, lame_any, bounds_any, hist_any, most_ref, spread_ref,
    disp_ref, mat_ref, lame_ref, bounds_ref, hist_ref, loaded,
    turned, send, own, faces, halos, rows_ref, halo_rows, moduli, weights, factors, cells,
    rhs_in, shear_in, rhs_two, shear_two, rhs_out, shear_out, factors_two, factors_shear,
    sent, got, face_sent, face_got,
):
    case = lax.axis_index("case")
    bx = lax.axis_index("bx")
    by = lax.axis_index("by")
    bricks = lax.axis_size("bx")
    slots = lax.axis_size("case")
    x_next = {"bx": lax.rem(bx + 1, bricks)}
    x_prev = {"bx": lax.rem(bx + bricks - 1, bricks)}
    partner = {"by": 1 - by}
    groups = slots // GROUP
    group = case // GROUP

    def relative(source, target):
        return lax.rem(source - target + groups, groups)

    above = {"case": lax.rem(case + 1, slots)}
    below = {"case": lax.rem(case + slots - 1, slots)}

    barrier = pltpu.get_barrier_semaphore()
    for target in range(slots):
        @pl.when(target != case)
        def _():
            pl.semaphore_signal(barrier, inc=1, device_id={"case": target}, device_id_type=MESH)
    for target in (x_next, x_prev, partner):
        pl.semaphore_signal(barrier, inc=1, device_id=target, device_id_type=MESH)

    loads = [
        pltpu.make_async_copy(src, dst, loaded.at[i])
        for i, (src, dst) in enumerate(
            (
                (disp_any, disp_ref),
                (hist_any, hist_ref),
                (mat_any, mat_ref),
                (lame_any, lame_ref),
                (bounds_any, bounds_ref),
            )
        )
    ]
    for load in loads:
        load.start()

    loads[0].wait()
    for a in range(3):
        first = disp_ref[0, a].astype(F32).reshape(64, 256)
        second = disp_ref[1, a].astype(F32).reshape(64, 256)
        turned[...] = jnp.concatenate([first, second], axis=0).T
        send[:, a] = turned[...].reshape(slots, 8, 128).astype(BF16)

    pl.semaphore_wait(barrier, slots + 2)
    mine = pltpu.make_async_copy(send.at[case], own.at[lax.rem(case, GROUP)], got.at[0])
    mine.start()
    for target in range(slots):
        @pl.when(target != case)
        def _():
            place = relative(group, target // GROUP)
            pltpu.make_async_remote_copy(
                src_ref=send.at[target],
                dst_ref=own.at[place * GROUP + lax.rem(case, GROUP)],
                send_sem=sent,
                recv_sem=got.at[place],
                device_id={"case": target},
                device_id_type=MESH,
            ).start()

    loads[1].wait()
    r = lax.broadcasted_iota(jnp.int32, (64, 128), 0)
    c = lax.broadcasted_iota(jnp.int32, (64, 128), 1)
    source = (c // (2 * GROUP) + group) % groups * GROUP + c % GROUP
    permute = (r == 2 * source + (c // GROUP) % 2).astype(F32).astype(BF16)
    steps = hist_ref.shape[1]
    for begin in range(0, steps, 256):
        block = hist_ref[:, begin : begin + 256].astype(F32).T.astype(BF16)
        factors[begin : begin + 256, :] = jnp.dot(
            block, permute, preferred_element_type=F32
        ).astype(BF16)

    half = steps // 2
    near = lax.broadcasted_iota(jnp.int32, (half, 128), 1) < 64
    early, late = factors[0:half, :], factors[half:steps, :]
    factors_two[:, 0:128] = early
    factors_two[:, 128:256] = late
    factors_shear[...] = jnp.where(near, early.astype(F32), late.astype(F32)).astype(BF16)
    rhs_two[...] = jnp.zeros(rhs_two.shape, BF16)
    shear_two[...] = jnp.zeros(shear_two.shape, BF16)

    for load in loads[2:]:
        load.wait()
    flat = mat_ref[...].astype(F32).reshape(64, 256)
    moduli[...] = jnp.concatenate([flat, flat], axis=0).T
    phase = moduli[pl.ds(pl.multiple_of(8 * case, 8), 8), :].astype(jnp.int32)
    lane = lax.broadcasted_iota(jnp.int32, (8, 128), 1)
    row = lax.broadcasted_iota(jnp.int32, (8, 128), 0)
    level = row + 8 * case
    column = (lane // 8) % 8
    shear_mod = jnp.zeros((8, 128), F32)
    lame_first = jnp.zeros((8, 128), F32)
    bottom = jnp.zeros((8, 128), jnp.int32)
    top = jnp.zeros((8, 128), jnp.int32)
    for m in range(8):
        shear_mod = jnp.where(phase == m, lame_ref[0, m], shear_mod)
        lame_first = jnp.where(phase == m, lame_ref[1, m], lame_first)
        bottom = jnp.where(column == m, bounds_ref[0, m], bottom)
        top = jnp.where(column == m, bounds_ref[1, m], top)
    weight = ((bottom <= level) & (level < top)).astype(F32)
    shear_mod = shear_mod * weight
    lame_first = lame_first * weight
    double = 2.0 * shear_mod

    r = lax.broadcasted_iota(jnp.int32, (128, 128), 0)
    c = lax.broadcasted_iota(jnp.int32, (128, 128), 1)
    cx = (c // 8) % 8
    cy = c % 8
    same = r // 64 == c // 64

    def picked(plus, minus):
        return jnp.where(plus, 0.5, jnp.where(minus, -0.5, 0.0)).astype(BF16)

    never = r < 0
    has_low = jnp.full((128, 128), bx, jnp.int32) > 0
    has_high = jnp.full((128, 128), bx, jnp.int32) < bricks - 1
    upper = jnp.full((128, 128), by, jnp.int32) > 0
    lower = jnp.full((128, 128), by, jnp.int32) < 1
    none = jnp.zeros((128, 128), BF16)
    weights[0:128, 0:128] = picked((r == c + 8) & (cx < 7), (r == c - 8) & (cx > 0))
    weights[0:128, 128:256] = picked((r == c + 1) & (cy < 7), (r == c - 1) & (cy > 0))
    alike = same & ((r // 8) % 8 == cx)
    weights[128:256, 0:128] = none
    weights[128:256, 128:256] = picked(alike & (cy == 7) & lower, alike & (cy == 0) & upper)
    weights[256:384, 0:128] = picked(never, same & (r % 8 == cy) & (cx == 0) & has_low)
    weights[384:512, 0:128] = picked(same & (r % 8 == cy) & (cx == 7) & has_high, never)
    weights[256:512, 128:256] = jnp.zeros((256, 128), BF16)

    in_upper = jnp.full((GROUP, 128), by, jnp.int32) > 0
    moves = {}

    @pl.when(case == 0)
    def _():
        halos[:, 3] = jnp.zeros(halos.shape[:1] + halos.shape[2:], BF16)

    @pl.when(case == slots - 1)
    def _():
        halos[:, 4] = jnp.zeros(halos.shape[:1] + halos.shape[2:], BF16)

    for g in order:
        s0 = GROUP * g
        arrived = own.at[pl.ds(s0, GROUP)]
        pltpu.make_async_remote_copy(
            src_ref=arrived, dst_ref=arrived, send_sem=sent, recv_sem=got.at[g],
            device_id=partner, device_id_type=MESH,
        ).wait_recv()
        rows_ref[g] = own[s0 : s0 + GROUP].astype(F32).reshape(24 * GROUP, 128)
        packed = [[], [], [], [], []]
        for a in range(3):
            to_next = to_prev = to_side = jnp.zeros((GROUP, 128), F32)
            for z in range(8):
                value = rows_ref[g, pl.ds(8 * a + z, GROUP, stride=24), :]
                to_next = jnp.where(column == z, pltpu.roll(value, (8 * z - 56) % 128, 1), to_next)
                to_prev = jnp.where(column == z, pltpu.roll(value, 8 * z, 1), to_prev)
                turn = jnp.where(in_upper, pltpu.roll(value, z, 1), pltpu.roll(value, (z - 7) % 128, 1))
                to_side = jnp.where(lane % 8 == z, turn, to_side)
                if z == 0:
                    packed[4].append(value)
                if z == 7:
                    packed[3].append(value)
            packed[0].append(to_next)
            packed[1].append(to_prev)
            packed[2].append(to_side)
        for k, target in enumerate((x_next, x_prev, partner, above, below)):
            for a in range(3):
                faces[g, k, a] = packed[k][a].astype(BF16)
            place = g
            if k >= 3:
                place = lax.rem(g + relative(group, target["case"] // GROUP), groups)
            move = pltpu.make_async_remote_copy(
                src_ref=faces.at[g, k],
                dst_ref=halos.at[place, k],
                send_sem=face_sent.at[g, k],
                recv_sem=face_got.at[place, k],
                device_id=target,
                device_id_type=MESH,
            )
            moves[g, k] = move
            if k < 3:
                move.start()
            elif k == 3:
                pl.when(case < slots - 1)(move.start)
            else:
                pl.when(case > 0)(move.start)

    in_column = column == row
    in_row = lane % 8 == row
    left = lane < 64

    def fetch(g, kinds):
        for k in kinds:
            arrival = pltpu.make_async_remote_copy(
                src_ref=faces.at[g, k], dst_ref=halos.at[g, k], send_sem=face_sent.at[g, k],
                recv_sem=face_got.at[g, k], device_id=partner, device_id_type=MESH,
            ).wait_recv
            if k < 3:
                arrival()
            elif k == 3:
                pl.when(case > 0)(arrival)
            else:
                pl.when(case < slots - 1)(arrival)
            halo_rows[g, k] = halos[g, k].astype(F32).reshape(3 * GROUP, 128)

    def stresses(g, full):
        def halo(k, i, a):
            at = GROUP * a + i
            return jnp.broadcast_to(halo_rows[g, k, at : at + 1, :], (8, 128))

        parts = [rows_ref[g]]
        for k, mask in ((2, in_row), (0, in_column), (1, in_column))[: 3 if full else 1]:
            parts.append(
                jnp.concatenate(
                    [
                        jnp.where(mask, halo(k, i, a), 0.0)
                        for i in range(GROUP)
                        for a in range(3)
                    ],
                    axis=0,
                )
            )
        flat = jnp.concatenate([part.astype(BF16) for part in parts], axis=1)
        planar = jnp.dot(flat, weights[0 : flat.shape[1], :], preferred_element_type=F32)
        for i in range(GROUP):
            grads = []
            for a in range(3):
                at = 24 * i + 8 * a
                field = rows_ref[g, at : at + 8]
                down = pltpu.roll(field, 1, 0)
                up = pltpu.roll(field, 7, 0)
                if full:
                    down = jnp.where(row == 0, halo(3, i, a), down)
                    up = jnp.where(row == 7, halo(4, i, a), up)
                grads.append(
                    (planar[at : at + 8, 0:128], planar[at : at + 8, 128:256], 0.5 * (up - down))
                )
            g_xx, g_yy, g_zz = grads[0][0], grads[1][1], grads[2][2]
            spread = lame_first * (g_xx + g_yy + g_zz)
            s_x, s_y, s_z, s_xy, s_yz, s_zx = [
                value.astype(BF16).astype(F32)
                for value in (
                    spread + double * g_xx,
                    spread + double * g_yy,
                    spread + double * g_zz,
                    shear_mod * (grads[0][1] + grads[1][0]),
                    shear_mod * (grads[1][2] + grads[2][1]),
                    shear_mod * (grads[2][0] + grads[0][2]),
                )
            ]
            values = (
                0.5 * (s_x - s_y),
                (s_x + s_y - 2.0 * s_z) * (0.5 / math.sqrt(3.0)),
                s_x + s_y + s_z,
                s_xy,
                s_yz,
                s_zx,
            )
            for k in range(6):
                cells[g, k, pl.ds(i, 8, stride=GROUP), :] = values[k]

    def level_of(g, k, z):
        return cells[g, k, GROUP * z : GROUP * (z + 1)]

    def keep(g, k, first, second, normal_ref, shear_ref, spots):
        both = jnp.concatenate([first, second], axis=0)
        coarse = both.astype(BF16)
        fine = (both - coarse.astype(F32)).astype(BF16)
        rows_here = 2 * GROUP
        for down, at in spots:
            begin = rows_here * g + down * (2 if k < 3 else 1)
            if k < 3:
                normal_ref[k, begin : begin + rows_here, at : at + 128] = coarse
                normal_ref[k, 64 + begin : 64 + begin + rows_here, at : at + 128] = fine
            else:
                shear_ref[k - 3, begin : begin + rows_here, at : at + 128] = coarse

    def pair_up(g, k, z_first, z_second, normal_ref, shear_ref, spots):
        one, two = level_of(g, k, z_first), level_of(g, k, z_second)
        first = jnp.where(left, one, pltpu.roll(two, 64, 1))
        second = jnp.where(left, pltpu.roll(one, 64, 1), two)
        keep(g, k, first, second, normal_ref, shear_ref, spots)

    def inner_columns(g):
        for k in range(6):
            pair_up(g, k, 1, 2, rhs_in, shear_in, ((0, 0),))
            pair_up(g, k, 3, 4, rhs_in, shear_in, ((0, 128),))
            pair_up(g, k, 5, 6, rhs_two, shear_two, ((0, 0), (64, 128)))

    def outer_columns(g):
        for k in range(6):
            pair_up(g, k, 0, 7, rhs_out, shear_out, ((0, 0),))
            first = second = jnp.zeros((GROUP, 128), F32)
            for z in range(1, 7):
                one = level_of(g, k, z)
                for side in range(2):
                    here = lane // 8 == 8 * side + z
                    turn = 8 * z + 8 * side
                    first = jnp.where(here, pltpu.roll(one, turn % 128, 1), first)
                    second = jnp.where(here, pltpu.roll(one, (turn - 64) % 128, 1), second)
            keep(g, k, first, second, rhs_out, shear_out, ((0, 128),))

    def extremes(lhs_ref, lhs_shear_ref, normal_ref, shear_ref):
        width = 256
        deep = shear_ref.shape[1]
        block = min(BLOCK, lhs_ref.shape[0])

        def body(i, carry):
            most, upper_h, lower_h = carry
            here = pl.ds(pl.multiple_of(i * block, block), block)
            full = lhs_ref[here, :]
            thin = lhs_shear_ref[here, 0:deep]
            total = None
            for k in (0, 1):
                part = jnp.dot(full, normal_ref[k], preferred_element_type=F32)
                total = part * part if total is None else total + part * part
            for k in range(3):
                part = jnp.dot(thin, shear_ref[k], preferred_element_type=F32)
                total = total + part * part
            mean = jnp.dot(full, normal_ref[2], preferred_element_type=F32)
            total = total.reshape(block // 8, 8, width)
            mean = mean.reshape(block // 8, 8, width)
            return (
                jnp.maximum(most, jnp.max(total, axis=0)),
                jnp.maximum(upper_h, jnp.max(mean, axis=0)),
                jnp.minimum(lower_h, jnp.min(mean, axis=0)),
            )

        start = (
            jnp.zeros((8, width), F32),
            jnp.full((8, width), -jnp.inf, F32),
            jnp.full((8, width), jnp.inf, F32),
        )
        most, upper_h, lower_h = lax.fori_loop(0, lhs_ref.shape[0] // block, body, start)
        most = jnp.max(most, axis=0, keepdims=True)
        upper_h = jnp.max(upper_h, axis=0, keepdims=True)
        lower_h = jnp.min(lower_h, axis=0, keepdims=True)
        return (most, upper_h, lower_h)

    for g in order:
        fetch(g, (2,))
        stresses(g, False)
        inner_columns(g)
    most, upper_h, lower_h = extremes(factors, factors, rhs_in, shear_in)
    inner = [(most, upper_h - lower_h)]
    most, upper_h, lower_h = extremes(factors_two, factors_shear, rhs_two, shear_two)
    inner.append(
        (
            jnp.maximum(most[:, 0:128], most[:, 128:256]),
            jnp.maximum(upper_h[:, 0:128], upper_h[:, 128:256])
            - jnp.minimum(lower_h[:, 0:128], lower_h[:, 128:256]),
        )
    )
    for g in order:
        fetch(g, (0, 1, 3, 4))
        stresses(g, True)
        outer_columns(g)
    most, upper_h, lower_h = extremes(factors, factors, rhs_out, shear_out)
    outer = (most, upper_h - lower_h)

    spot = lax.broadcasted_iota(jnp.int32, (1, 128), 1)
    for which, out_ref in ((0, most_ref), (1, spread_ref)):
        ends = outer[which][:, 0:128]
        sides = outer[which][:, 128:256]
        pairs = [inner[0][which][:, 0:128], inner[0][which][:, 128:256], inner[1][which]]
        rows = [ends]
        for z in range(1, 7):
            line = pairs[(z - 1) // 2]
            if z % 2 == 0:
                line = pltpu.roll(line, 64, 1)
            line = jnp.where(spot < 8, pltpu.roll(sides, -8 * z % 128, 1), line)
            line = jnp.where(spot >= 56, pltpu.roll(sides, (-8 * z - 8) % 128, 1), line)
            rows.append(line)
        rows.append(pltpu.roll(ends, 64, 1))
        out_ref[...] = jnp.concatenate(rows, axis=0).T[0:64].reshape(8, 8, 8)

    whole = send.at[pl.ds(0, slots - 1)]
    pltpu.make_async_remote_copy(
        src_ref=whole, dst_ref=whole, send_sem=sent, recv_sem=got.at[0],
        device_id=partner, device_id_type=MESH,
    ).wait_send()
    for (_, k), move in moves.items():
        if k < 3:
            move.wait_send()
        elif k == 3:
            pl.when(case < slots - 1)(move.wait_send)
        else:
            pl.when(case > 0)(move.wait_send)


def shards(displacements, material_ids, lame, slab_bounds, load_history):
    slots = lax.axis_size("case")
    groups = slots // GROUP
    steps = load_history.shape[0]
    anywhere = pl.BlockSpec(memory_space=pl.ANY)
    vmem = pl.BlockSpec(memory_space=pltpu.VMEM)
    shape = jax.ShapeDtypeStruct((8, 8, 8), F32)
    factors = load_history.T
    most, spread = pl.pallas_call(
        functools.partial(kernel, (0, 1, 3, 2)),
        out_shape=(shape, shape),
        in_specs=[anywhere] * 5,
        out_specs=(vmem, vmem),
        scratch_shapes=[
            pltpu.VMEM(displacements.shape, BF16),
            pltpu.VMEM(material_ids.shape, jnp.int32),
            pltpu.SMEM(lame.shape, F32),
            pltpu.SMEM(slab_bounds.shape, jnp.int32),
            pltpu.VMEM(factors.shape, BF16),
            pltpu.SemaphoreType.DMA((5,)),
            pltpu.VMEM((256, 128), F32),
            pltpu.VMEM((slots, 3, 8, 128), BF16),
            pltpu.VMEM((slots, 3, 8, 128), BF16),
            pltpu.VMEM((groups, 5, 3, GROUP, 128), BF16),
            pltpu.VMEM((groups, 5, 3, GROUP, 128), BF16),
            pltpu.VMEM((groups, 24 * GROUP, 128), F32),
            pltpu.VMEM((groups, 5, 3 * GROUP, 128), F32),
            pltpu.VMEM((256, 128), F32),
            pltpu.VMEM((512, 256), BF16),
            pltpu.VMEM((steps, 128), BF16),
            pltpu.VMEM((groups, 6, 8 * GROUP, 128), F32),
            pltpu.VMEM((3, 128, 256), BF16),
            pltpu.VMEM((3, 64, 256), BF16),
            pltpu.VMEM((3, 256, 256), BF16),
            pltpu.VMEM((3, 128, 256), BF16),
            pltpu.VMEM((3, 128, 256), BF16),
            pltpu.VMEM((3, 64, 256), BF16),
            pltpu.VMEM((steps // 2, 256), BF16),
            pltpu.VMEM((steps // 2, 128), BF16),
            pltpu.SemaphoreType.DMA,
            pltpu.SemaphoreType.DMA((groups,)),
            pltpu.SemaphoreType.DMA((groups, 5)),
            pltpu.SemaphoreType.DMA((groups, 5)),
        ],
        compiler_params=pltpu.CompilerParams(collective_id=0, has_side_effects=True, vmem_limit_bytes=32768 * 1024),

    )(*[pltpu.with_memory_space_constraint(v, pltpu.MemorySpace.HBM) for v in (displacements, material_ids, lame, slab_bounds, factors)])
    return (jnp.sqrt(3.0 * most), spread * (1.0 / 3.0))


def solution(mesh):
    in_specs = (P("case", None, "bx", "by", None), P("bx", "by", None), P(), P(None, "bx"), P())
    out_specs = (P("bx", "by", "case"), P("bx", "by", "case"))
    return jax.shard_map(shards, mesh=mesh, in_specs=in_specs, out_specs=out_specs, check_vma=False)
```

```python
import functools
import math

import jax
import jax.numpy as jnp
from jax import lax
from jax.experimental import pallas as pl
from jax.experimental.pallas import tpu as pltpu
from jax.sharding import PartitionSpec as P

MESH = pl.DeviceIdType.MESH
F32 = jnp.float32
BF16 = jnp.bfloat16
GROUP = 8
BLOCK = 1024


def kernel(
    order, disp_any, mat_any, lame_any, bounds_any, hist_any, most_ref, spread_ref,
    disp_ref, mat_ref, lame_ref, bounds_ref, hist_ref, loaded,
    turned, send, own, faces, halos, rows_ref, halo_rows, moduli, weights, factors, cells,
    rhs_in, shear_in, rhs_two, shear_two, rhs_out, shear_out, factors_two, factors_shear,
    sent, got, face_sent, face_got,
):
    case = lax.axis_index("case")
    bx = lax.axis_index("bx")
    by = lax.axis_index("by")
    bricks = lax.axis_size("bx")
    slots = lax.axis_size("case")
    x_next = {"bx": lax.rem(bx + 1, bricks)}
    x_prev = {"bx": lax.rem(bx + bricks - 1, bricks)}
    partner = {"by": 1 - by}
    groups = slots // GROUP
    group = case // GROUP

    def relative(source, target):
        return lax.rem(source - target + groups, groups)

    above = {"case": lax.rem(case + 1, slots)}
    below = {"case": lax.rem(case + slots - 1, slots)}

    barrier = pltpu.get_barrier_semaphore()
    for target in range(slots):
        @pl.when(target != case)
        def _():
            pl.semaphore_signal(barrier, inc=1, device_id={"case": target}, device_id_type=MESH)
    for target in (x_next, x_prev, partner):
        pl.semaphore_signal(barrier, inc=1, device_id=target, device_id_type=MESH)

    loads = [
        pltpu.make_async_copy(src, dst, loaded.at[i])
        for i, (src, dst) in enumerate(
            (
                (disp_any, disp_ref),
                (hist_any, hist_ref),
                (mat_any, mat_ref),
                (lame_any, lame_ref),
                (bounds_any, bounds_ref),
            )
        )
    ]
    for load in loads:
        load.start()

    loads[0].wait()
    for a in range(3):
        first = disp_ref[0, a].astype(F32).reshape(64, 256)
        second = disp_ref[1, a].astype(F32).reshape(64, 256)
        turned[...] = jnp.concatenate([first, second], axis=0).T
        send[:, a] = turned[...].reshape(slots, 8, 128).astype(BF16)

    pl.semaphore_wait(barrier, slots + 2)
    mine = pltpu.make_async_copy(send.at[case], own.at[lax.rem(case, GROUP)], got.at[0])
    mine.start()
    for target in range(slots):
        @pl.when(target != case)
        def _():
            place = relative(group, target // GROUP)
            pltpu.make_async_remote_copy(
                src_ref=send.at[target],
                dst_ref=own.at[place * GROUP + lax.rem(case, GROUP)],
                send_sem=sent,
                recv_sem=got.at[place],
                device_id={"case": target},
                device_id_type=MESH,
            ).start()

    loads[1].wait()
    r = lax.broadcasted_iota(jnp.int32, (64, 128), 0)
    c = lax.broadcasted_iota(jnp.int32, (64, 128), 1)
    source = (c // (2 * GROUP) + group) % groups * GROUP + c % GROUP
    permute = (r == 2 * source + (c // GROUP) % 2).astype(F32).astype(BF16)
    steps = hist_ref.shape[1]
    for begin in range(0, steps, 256):
        block = hist_ref[:, begin : begin + 256].astype(F32).T.astype(BF16)
        factors[begin : begin + 256, :] = jnp.dot(
            block, permute, preferred_element_type=F32
        ).astype(BF16)

    half = steps // 2
    near = lax.broadcasted_iota(jnp.int32, (half, 128), 1) < 64
    early, late = factors[0:half, :], factors[half:steps, :]
    factors_two[:, 0:128] = early
    factors_two[:, 128:256] = late
    factors_shear[...] = jnp.where(near, early.astype(F32), late.astype(F32)).astype(BF16)
    rhs_two[...] = jnp.zeros(rhs_two.shape, BF16)
    shear_two[...] = jnp.zeros(shear_two.shape, BF16)

    for load in loads[2:]:
        load.wait()
    flat = mat_ref[...].astype(F32).reshape(64, 256)
    moduli[...] = jnp.concatenate([flat, flat], axis=0).T
    phase = moduli[pl.ds(pl.multiple_of(8 * case, 8), 8), :].astype(jnp.int32)
    lane = lax.broadcasted_iota(jnp.int32, (8, 128), 1)
    row = lax.broadcasted_iota(jnp.int32, (8, 128), 0)
    level = row + 8 * case
    column = (lane // 8) % 8
    shear_mod = jnp.zeros((8, 128), F32)
    lame_first = jnp.zeros((8, 128), F32)
    bottom = jnp.zeros((8, 128), jnp.int32)
    top = jnp.zeros((8, 128), jnp.int32)
    for m in range(8):
        shear_mod = jnp.where(phase == m, lame_ref[0, m], shear_mod)
        lame_first = jnp.where(phase == m, lame_ref[1, m], lame_first)
        bottom = jnp.where(column == m, bounds_ref[0, m], bottom)
        top = jnp.where(column == m, bounds_ref[1, m], top)
    weight = ((bottom <= level) & (level < top)).astype(F32)
    shear_mod = shear_mod * weight
    lame_first = lame_first * weight
    double = 2.0 * shear_mod

    r = lax.broadcasted_iota(jnp.int32, (128, 128), 0)
    c = lax.broadcasted_iota(jnp.int32, (128, 128), 1)
    cx = (c // 8) % 8
    cy = c % 8
    same = r // 64 == c // 64

    def picked(plus, minus):
        return jnp.where(plus, 0.5, jnp.where(minus, -0.5, 0.0)).astype(BF16)

    never = r < 0
    has_low = jnp.full((128, 128), bx, jnp.int32) > 0
    has_high = jnp.full((128, 128), bx, jnp.int32) < bricks - 1
    upper = jnp.full((128, 128), by, jnp.int32) > 0
    lower = jnp.full((128, 128), by, jnp.int32) < 1
    none = jnp.zeros((128, 128), BF16)
    weights[0:128, 0:128] = picked((r == c + 8) & (cx < 7), (r == c - 8) & (cx > 0))
    weights[0:128, 128:256] = picked((r == c + 1) & (cy < 7), (r == c - 1) & (cy > 0))
    alike = same & ((r // 8) % 8 == cx)
    weights[128:256, 0:128] = none
    weights[128:256, 128:256] = picked(alike & (cy == 7) & lower, alike & (cy == 0) & upper)
    weights[256:384, 0:128] = picked(never, same & (r % 8 == cy) & (cx == 0) & has_low)
    weights[384:512, 0:128] = picked(same & (r % 8 == cy) & (cx == 7) & has_high, never)
    weights[256:512, 128:256] = jnp.zeros((256, 128), BF16)

    in_upper = jnp.full((GROUP, 128), by, jnp.int32) > 0
    moves = {}

    @pl.when(case == 0)
    def _():
        halos[:, 3] = jnp.zeros(halos.shape[:1] + halos.shape[2:], BF16)

    @pl.when(case == slots - 1)
    def _():
        halos[:, 4] = jnp.zeros(halos.shape[:1] + halos.shape[2:], BF16)

    for g in order:
        s0 = GROUP * g
        arrived = own.at[pl.ds(s0, GROUP)]
        pltpu.make_async_remote_copy(
            src_ref=arrived, dst_ref=arrived, send_sem=sent, recv_sem=got.at[g],
            device_id=partner, device_id_type=MESH,
        ).wait_recv()
        rows_ref[g] = own[s0 : s0 + GROUP].astype(F32).reshape(24 * GROUP, 128)
        values = [
            [rows_ref[g, pl.ds(8 * a + z, GROUP, stride=24), :] for z in range(8)] for a in range(3)
        ]

        def face(k, a):
            if k >= 3:
                return values[a][7 if k == 3 else 0]
            total = jnp.zeros((GROUP, 128), F32)
            for z, value in enumerate(values[a]):
                if k == 2:
                    turn = jnp.where(
                        in_upper, pltpu.roll(value, z, 1), pltpu.roll(value, (z - 7) % 128, 1)
                    )
                    total = jnp.where(lane % 8 == z, turn, total)
                else:
                    turn = pltpu.roll(value, (8 * z - 56 * (1 - k)) % 128, 1)
                    total = jnp.where(column == z, turn, total)
            return total

        for k, target in ((3, above), (4, below), (0, x_next), (1, x_prev), (2, partner)):
            for a in range(3):
                faces[g, k, a] = face(k, a).astype(BF16)
            place = g
            if k >= 3:
                place = lax.rem(g + relative(group, target["case"] // GROUP), groups)
            move = pltpu.make_async_remote_copy(
                src_ref=faces.at[g, k],
                dst_ref=halos.at[place, k],
                send_sem=face_sent.at[g, k],
                recv_sem=face_got.at[place, k],
                device_id=target,
                device_id_type=MESH,
            )
            moves[g, k] = move
            if k < 3:
                move.start()
            elif k == 3:
                pl.when(case < slots - 1)(move.start)
            else:
                pl.when(case > 0)(move.start)

    in_column = column == row
    in_row = lane % 8 == row
    left = lane < 64

    def fetch(g, kinds):
        for k in kinds:
            arrival = pltpu.make_async_remote_copy(
                src_ref=faces.at[g, k], dst_ref=halos.at[g, k], send_sem=face_sent.at[g, k],
                recv_sem=face_got.at[g, k], device_id=partner, device_id_type=MESH,
            ).wait_recv
            if k < 3:
                arrival()
            elif k == 3:
                pl.when(case > 0)(arrival)
            else:
                pl.when(case < slots - 1)(arrival)
            halo_rows[g, k] = halos[g, k].astype(F32).reshape(3 * GROUP, 128)

    def stresses(g, full):
        def halo(k, i, a):
            at = GROUP * a + i
            return jnp.broadcast_to(halo_rows[g, k, at : at + 1, :], (8, 128))

        parts = [rows_ref[g]]
        for k, mask in ((2, in_row), (0, in_column), (1, in_column))[: 3 if full else 1]:
            parts.append(
                jnp.concatenate(
                    [
                        jnp.where(mask, halo(k, i, a), 0.0)
                        for i in range(GROUP)
                        for a in range(3)
                    ],
                    axis=0,
                )
            )
        flat = jnp.concatenate([part.astype(BF16) for part in parts], axis=1)
        planar = jnp.dot(flat, weights[0 : flat.shape[1], :], preferred_element_type=F32)
        for i in range(GROUP):
            grads = []
            for a in range(3):
                at = 24 * i + 8 * a
                field = rows_ref[g, at : at + 8]
                down = pltpu.roll(field, 1, 0)
                up = pltpu.roll(field, 7, 0)
                if full:
                    down = jnp.where(row == 0, halo(3, i, a), down)
                    up = jnp.where(row == 7, halo(4, i, a), up)
                grads.append(
                    (planar[at : at + 8, 0:128], planar[at : at + 8, 128:256], 0.5 * (up - down))
                )
            g_xx, g_yy, g_zz = grads[0][0], grads[1][1], grads[2][2]
            spread = lame_first * (g_xx + g_yy + g_zz)
            s_x, s_y, s_z, s_xy, s_yz, s_zx = [
                value.astype(BF16).astype(F32)
                for value in (
                    spread + double * g_xx,
                    spread + double * g_yy,
                    spread + double * g_zz,
                    shear_mod * (grads[0][1] + grads[1][0]),
                    shear_mod * (grads[1][2] + grads[2][1]),
                    shear_mod * (grads[2][0] + grads[0][2]),
                )
            ]
            values = (
                0.5 * (s_x - s_y),
                (s_x + s_y - 2.0 * s_z) * (0.5 / math.sqrt(3.0)),
                s_x + s_y + s_z,
                s_xy,
                s_yz,
                s_zx,
            )
            for k in range(6):
                cells[g, k, pl.ds(i, 8, stride=GROUP), :] = values[k]

    def level_of(g, k, z):
        return cells[g, k, GROUP * z : GROUP * (z + 1)]

    def keep(g, k, first, second, normal_ref, shear_ref, spots):
        both = jnp.concatenate([first, second], axis=0)
        coarse = both.astype(BF16)
        fine = (both - coarse.astype(F32)).astype(BF16)
        rows_here = 2 * GROUP
        for down, at in spots:
            begin = rows_here * g + down * (2 if k < 3 else 1)
            if k < 3:
                normal_ref[k, begin : begin + rows_here, at : at + 128] = coarse
                normal_ref[k, 64 + begin : 64 + begin + rows_here, at : at + 128] = fine
            else:
                shear_ref[k - 3, begin : begin + rows_here, at : at + 128] = coarse

    def pair_up(g, k, z_first, z_second, normal_ref, shear_ref, spots):
        one, two = level_of(g, k, z_first), level_of(g, k, z_second)
        first = jnp.where(left, one, pltpu.roll(two, 64, 1))
        second = jnp.where(left, pltpu.roll(one, 64, 1), two)
        keep(g, k, first, second, normal_ref, shear_ref, spots)

    def inner_columns(g):
        for k in range(6):
            pair_up(g, k, 1, 2, rhs_in, shear_in, ((0, 0),))
            pair_up(g, k, 3, 4, rhs_in, shear_in, ((0, 128),))
            pair_up(g, k, 5, 6, rhs_two, shear_two, ((0, 0), (64, 128)))

    def outer_columns(g):
        for k in range(6):
            pair_up(g, k, 0, 7, rhs_out, shear_out, ((0, 0),))
            first = second = jnp.zeros((GROUP, 128), F32)
            for z in range(1, 7):
                one = level_of(g, k, z)
                for side in range(2):
                    here = lane // 8 == 8 * side + z
                    turn = 8 * z + 8 * side
                    first = jnp.where(here, pltpu.roll(one, turn % 128, 1), first)
                    second = jnp.where(here, pltpu.roll(one, (turn - 64) % 128, 1), second)
            keep(g, k, first, second, rhs_out, shear_out, ((0, 128),))

    def extremes(lhs_ref, lhs_shear_ref, normal_ref, shear_ref):
        width = 256
        deep = shear_ref.shape[1]
        block = min(BLOCK, lhs_ref.shape[0])

        def body(i, carry):
            most, upper_h, lower_h = carry
            here = pl.ds(pl.multiple_of(i * block, block), block)
            full = lhs_ref[here, :]
            thin = lhs_shear_ref[here, 0:deep]
            total = None
            for k in (0, 1):
                part = jnp.dot(full, normal_ref[k], preferred_element_type=F32)
                total = part * part if total is None else total + part * part
            for k in range(3):
                part = jnp.dot(thin, shear_ref[k], preferred_element_type=F32)
                total = total + part * part
            mean = jnp.dot(full, normal_ref[2], preferred_element_type=F32)
            total = total.reshape(block // 8, 8, width)
            mean = mean.reshape(block // 8, 8, width)
            return (
                jnp.maximum(most, jnp.max(total, axis=0)),
                jnp.maximum(upper_h, jnp.max(mean, axis=0)),
                jnp.minimum(lower_h, jnp.min(mean, axis=0)),
            )

        start = (
            jnp.zeros((8, width), F32),
            jnp.full((8, width), -jnp.inf, F32),
            jnp.full((8, width), jnp.inf, F32),
        )
        most, upper_h, lower_h = lax.fori_loop(0, lhs_ref.shape[0] // block, body, start)
        most = jnp.max(most, axis=0, keepdims=True)
        upper_h = jnp.max(upper_h, axis=0, keepdims=True)
        lower_h = jnp.min(lower_h, axis=0, keepdims=True)
        return (most, upper_h, lower_h)

    for g in order:
        fetch(g, (2,))
        stresses(g, False)
        inner_columns(g)
    most, upper_h, lower_h = extremes(factors, factors, rhs_in, shear_in)
    inner = [(most, upper_h - lower_h)]
    most, upper_h, lower_h = extremes(factors_two, factors_shear, rhs_two, shear_two)
    inner.append(
        (
            jnp.maximum(most[:, 0:128], most[:, 128:256]),
            jnp.maximum(upper_h[:, 0:128], upper_h[:, 128:256])
            - jnp.minimum(lower_h[:, 0:128], lower_h[:, 128:256]),
        )
    )
    for g in order:
        fetch(g, (0, 1, 3, 4))
        stresses(g, True)
        outer_columns(g)
    most, upper_h, lower_h = extremes(factors, factors, rhs_out, shear_out)
    outer = (most, upper_h - lower_h)

    spot = lax.broadcasted_iota(jnp.int32, (1, 128), 1)
    for which, out_ref in ((0, most_ref), (1, spread_ref)):
        ends = outer[which][:, 0:128]
        sides = outer[which][:, 128:256]
        pairs = [inner[0][which][:, 0:128], inner[0][which][:, 128:256], inner[1][which]]
        rows = [ends]
        for z in range(1, 7):
            line = pairs[(z - 1) // 2]
            if z % 2 == 0:
                line = pltpu.roll(line, 64, 1)
            line = jnp.where(spot < 8, pltpu.roll(sides, -8 * z % 128, 1), line)
            line = jnp.where(spot >= 56, pltpu.roll(sides, (-8 * z - 8) % 128, 1), line)
            rows.append(line)
        rows.append(pltpu.roll(ends, 64, 1))
        out_ref[...] = jnp.concatenate(rows, axis=0).T[0:64].reshape(8, 8, 8)

    whole = send.at[pl.ds(0, slots - 1)]
    pltpu.make_async_remote_copy(
        src_ref=whole, dst_ref=whole, send_sem=sent, recv_sem=got.at[0],
        device_id=partner, device_id_type=MESH,
    ).wait_send()
    for (_, k), move in moves.items():
        if k < 3:
            move.wait_send()
        elif k == 3:
            pl.when(case < slots - 1)(move.wait_send)
        else:
            pl.when(case > 0)(move.wait_send)


def shards(displacements, material_ids, lame, slab_bounds, load_history):
    slots = lax.axis_size("case")
    groups = slots // GROUP
    steps = load_history.shape[0]
    anywhere = pl.BlockSpec(memory_space=pl.ANY)
    vmem = pl.BlockSpec(memory_space=pltpu.VMEM)
    shape = jax.ShapeDtypeStruct((8, 8, 8), F32)
    factors = load_history.T
    most, spread = pl.pallas_call(
        functools.partial(kernel, (0, 1, 3, 2)),
        out_shape=(shape, shape),
        in_specs=[anywhere] * 5,
        out_specs=(vmem, vmem),
        scratch_shapes=[
            pltpu.VMEM(displacements.shape, BF16),
            pltpu.VMEM(material_ids.shape, jnp.int32),
            pltpu.SMEM(lame.shape, F32),
            pltpu.SMEM(slab_bounds.shape, jnp.int32),
            pltpu.VMEM(factors.shape, BF16),
            pltpu.SemaphoreType.DMA((5,)),
            pltpu.VMEM((256, 128), F32),
            pltpu.VMEM((slots, 3, 8, 128), BF16),
            pltpu.VMEM((slots, 3, 8, 128), BF16),
            pltpu.VMEM((groups, 5, 3, GROUP, 128), BF16),
            pltpu.VMEM((groups, 5, 3, GROUP, 128), BF16),
            pltpu.VMEM((groups, 24 * GROUP, 128), F32),
            pltpu.VMEM((groups, 5, 3 * GROUP, 128), F32),
            pltpu.VMEM((256, 128), F32),
            pltpu.VMEM((512, 256), BF16),
            pltpu.VMEM((steps, 128), BF16),
            pltpu.VMEM((groups, 6, 8 * GROUP, 128), F32),
            pltpu.VMEM((3, 128, 256), BF16),
            pltpu.VMEM((3, 64, 256), BF16),
            pltpu.VMEM((3, 256, 256), BF16),
            pltpu.VMEM((3, 128, 256), BF16),
            pltpu.VMEM((3, 128, 256), BF16),
            pltpu.VMEM((3, 64, 256), BF16),
            pltpu.VMEM((steps // 2, 256), BF16),
            pltpu.VMEM((steps // 2, 128), BF16),
            pltpu.SemaphoreType.DMA,
            pltpu.SemaphoreType.DMA((groups,)),
            pltpu.SemaphoreType.DMA((groups, 5)),
            pltpu.SemaphoreType.DMA((groups, 5)),
        ],
        compiler_params=pltpu.CompilerParams(collective_id=0, has_side_effects=True, vmem_limit_bytes=32768 * 1024),

    )(*[pltpu.with_memory_space_constraint(v, pltpu.MemorySpace.HBM) for v in (displacements, material_ids, lame, slab_bounds, factors)])
    return (jnp.sqrt(3.0 * most), spread * (1.0 / 3.0))


def solution(mesh):
    in_specs = (P("case", None, "bx", "by", None), P("bx", "by", None), P(), P(None, "bx"), P())
    out_specs = (P("bx", "by", "case"), P("bx", "by", "case"))
    return jax.shard_map(shards, mesh=mesh, in_specs=in_specs, out_specs=out_specs, check_vma=False)
```
